512 devices in a mesh: gx: 64 (over z, x, core), gy: 8 (over y).
Axes of the slice: x: 4, y: 8, z: 8, core: 2. Of those that a mesh axis runs over, the one named last changes fastest.
Arguments:
- velocity: float32 [3, 128, 1536, 128], P(None, 'gx', 'gy'), may hold values from -0.8 to 2.3
- stiffness: float32 [8], P('gy'), may hold values from 100 to 100000
- block_inverse: float32 [3, 1536, 192], P(None, 'gy'), as said below
Outputs:
- velocity_next: float32 [3, 128, 1536, 128], P(None, 'gx', 'gy')
The draws below stay inside these ranges and needn't reach their ends.
Inputs may be any that keep to these rules, and one draw needn't show every extreme that they name: block_inverse[s] for block k is, to float32 rounding, the inverse of the 192-row matrix with 1 + 2 b on its diagonal and -b beside it, b = alpha_s stiffness[k].
All inputs are finite; a program needn't handle non-finite values.
Results may differ from the reference program's by a relative error of at most 0.0003.
Values sent between devices are 32-bit elements; how exact they have to be, the bound alone decides.
No kernel may reach another device: no remote copies, remote signals or barrier semaphores. Data moves between devices by JAX's collectives and lax.ppermute only.
A program may use at most 64 MiB of HBM per device.

```python
import math
import jax
import jax.numpy as jnp
from jax import lax

CY = 192
NZ = 128
SUBSTEPS = 3
BLOCKS = 8
NX = 128
NY = 1536
N_GY = 8


def stiffness_values(key):
    order = jax.random.permutation(jax.random.fold_in(key, 11), BLOCKS)
    spread = jax.random.uniform(jax.random.fold_in(key, 12), (BLOCKS,), jnp.float32)
    level = (order.astype(jnp.float32) + spread) / BLOCKS
    return 100.0 * jnp.exp(level * math.log(1000.0))


def draw_velocity(key, part):
    rows = (jnp.arange(NY).astype(jnp.float32) + 0.5) / NY
    profile = jnp.sin(math.pi * rows)[None, None, :, None]
    rough = 0.2 * jnp.clip(jax.random.normal(jax.random.fold_in(key, 21), (3, NX, NY, NZ), jnp.float32), -4.0, 4.0)
    levels = jnp.array([1.5, 0.0, 0.0], jnp.float32)
    return levels[:, None, None, None] * profile + rough


def draw_stiffness(key, part):
    return stiffness_values(key)


def draw_block_inverse(key, part):
    values = stiffness_values(key)
    shares = jnp.array([8.0 / 15.0, 2.0 / 15.0, 1.0 / 3.0], jnp.float32)
    strength = (shares[:, None] * values[None, :])[:, :, None, None]
    half_ratio = 0.5 / jnp.sqrt(strength)
    squared = half_ratio * half_ratio
    theta = 2.0 * jnp.log1p(half_ratio + squared / (1.0 + jnp.sqrt(1.0 + squared)))
    rows = jnp.arange(1, CY + 1).astype(jnp.float32)
    smaller = jnp.minimum(rows[:, None], rows[None, :])
    larger = jnp.maximum(rows[:, None], rows[None, :])
    upper_part = jnp.sinh(smaller * theta) * jnp.sinh((CY + 1.0 - larger) * theta)
    lower_part = strength * jnp.sinh(theta) * jnp.sinh((CY + 1.0) * theta)
    table = upper_part / lower_part
    return table.reshape(3, BLOCKS * CY, CY).astype(jnp.float32)


def setup_inputs(seed: int = 0) -> dict:
    key_of = jax.random.split(jax.random.key(seed), 4)
    velocity = draw_velocity(jax.random.fold_in(key_of[3], 71), 0)
    stiffness = draw_stiffness(jax.random.fold_in(key_of[3], 71), 0)
    block_inverse = draw_block_inverse(jax.random.fold_in(key_of[3], 71), 0)
    return {"velocity": velocity, "stiffness": stiffness, "block_inverse": block_inverse}


implicit_share = (8.0 / 15.0, 2.0 / 15.0, 1.0 / 3.0)
new_weight = (8.0 / 15.0, 5.0 / 12.0, 3.0 / 4.0)
old_weight = (0.0, -17.0 / 60.0, -5.0 / 12.0)
courant = (0.3, 0.2, 0.3)


def upwind(field, back_two, back_one, ahead_one, ahead_two, speed):
    behind = 1.5 * field - 2.0 * back_one + 0.5 * back_two
    ahead = -1.5 * field + 2.0 * ahead_one - 0.5 * ahead_two
    return jnp.maximum(speed, 0.0) * behind + jnp.minimum(speed, 0.0) * ahead


def reduced(first_vals, last_vals, tips):
    count = first_vals.shape[0]
    prev_q = jnp.zeros((), jnp.float32)
    prev_last = jnp.zeros_like(first_vals[0])
    fronts, backs, front_qs, back_qs = [], [], [], []
    for block in range(count):
        head_v = tips[0][block]
        tail_v = tips[1][block]
        head_w = tips[2][block]
        tail_w = tips[3][block]
        pivot = 1.0 - head_v * prev_q
        front = (first_vals[block] - head_v * prev_last) / pivot
        back = last_vals[block] - tail_v * prev_last + tail_v * prev_q * front
        front_q = head_w / pivot
        back_q = tail_w + tail_v * prev_q * front_q
        fronts.append(front)
        backs.append(back)
        front_qs.append(front_q)
        back_qs.append(back_q)
        prev_q = back_q
        prev_last = back
    heads = [None] * count
    tails = [None] * count
    heads[count - 1] = fronts[count - 1]
    tails[count - 1] = backs[count - 1]
    for block in range(count - 2, -1, -1):
        after = heads[block + 1]
        heads[block] = fronts[block] - front_qs[block] * after
        tails[block] = backs[block] - back_qs[block] * after
    zero = jnp.zeros_like(first_vals[0])
    lower_prev = jnp.stack([zero] + tails[:-1])
    upper_next = jnp.stack(heads[1:] + [zero])
    return lower_prev, upper_next


def reference(velocity, stiffness, block_inverse):
    count = N_GY
    inverse = block_inverse.reshape(SUBSTEPS, count, CY, CY)
    block_ids = jnp.arange(count)
    first_flag = (block_ids > 0).astype(jnp.float32)
    last_flag = (block_ids < count - 1).astype(jnp.float32)
    row_stiff = jnp.repeat(stiffness, CY)[None, :, None]
    current = velocity
    previous = jnp.zeros_like(velocity)
    for step in range(SUBSTEPS):
        speed_x = current[0]
        speed_y = current[1]
        speed_z = current[2]

        def component(pair):
            field, earlier = pair
            along_x = upwind(field, jnp.roll(field, 2, 0), jnp.roll(field, 1, 0), jnp.roll(field, -1, 0), jnp.roll(field, -2, 0), speed_x)
            padded = jnp.pad(field, ((0, 0), (2, 2), (0, 0)))
            along_y = upwind(field, padded[:, 0:-4], padded[:, 1:-3], padded[:, 3:-1], padded[:, 4:], speed_y)
            along_z = upwind(field, jnp.roll(field, 2, 2), jnp.roll(field, 1, 2), jnp.roll(field, -1, 2), jnp.roll(field, -2, 2), speed_z)
            advect = courant[0] * along_x + courant[1] * along_y + courant[2] * along_z
            diffuse = row_stiff * (padded[:, 3:-1] - 2.0 * field + padded[:, 1:-3])
            forcing = field + implicit_share[step] * diffuse - new_weight[step] * advect - old_weight[step] * earlier
            return forcing, advect

        forcing, previous = lax.map(component, (current, previous))
        shaped = forcing.reshape(3, NX, count, CY, NZ)
        solved = jnp.einsum("kij,cxkjz->cxkiz", inverse[step], shaped, precision=lax.Precision.HIGHEST)
        coupling = -implicit_share[step] * stiffness
        lower = coupling * first_flag
        upper = coupling * last_flag
        column_v = inverse[step][:, :, 0] * lower[:, None]
        column_w = inverse[step][:, :, -1] * upper[:, None]
        tips = (column_v[:, 0], column_v[:, -1], column_w[:, 0], column_w[:, -1])
        first_vals = jnp.moveaxis(solved[:, :, :, 0, :], 2, 0)
        last_vals = jnp.moveaxis(solved[:, :, :, -1, :], 2, 0)
        lower_prev, upper_next = reduced(first_vals, last_vals, tips)
        lower_prev = jnp.moveaxis(lower_prev, 0, 2)[:, :, :, None, :]
        upper_next = jnp.moveaxis(upper_next, 0, 2)[:, :, :, None, :]
        result = solved - column_v[None, None, :, :, None] * lower_prev - column_w[None, None, :, :, None] * upper_next
        current = result.reshape(3, NX, NY, NZ)
    return current
```

```python
import functools

import jax
import jax.numpy as jnp
from jax import lax
from jax.experimental import pallas as pl
from jax.experimental.pallas import tpu as pltpu
from jax.sharding import PartitionSpec as P

SUBSTEPS = 3
implicit_share = (8.0 / 15.0, 2.0 / 15.0, 1.0 / 3.0)
new_weight = (8.0 / 15.0, 5.0 / 12.0, 3.0 / 4.0)
old_weight = (0.0, -17.0 / 60.0, -5.0 / 12.0)
courant = (0.3, 0.2, 0.3)

CY = 192
LANES = 128
CHUNK = 32
ENDS = (0, 1, CY - 2, CY - 1)

VMEM = pl.BlockSpec(memory_space=pltpu.VMEM)
SMEM = pl.BlockSpec(memory_space=pltpu.SMEM)


def swaps(count, offset, closed):
    pairs = []
    for a in range(offset, count + offset - 1, 2):
        b = a + 1
        if b < count:
            pairs += [(a, b), (b, a)]
        elif closed:
            pairs += [(a, 0), (0, a)]
    return pairs


def forcing_kernel(step, *refs):
    if step == 0:
        place, stiff_ref, u_ref, far, near, pair_y, other_y, inv_ref, *refs = refs
        old_ref = None
    else:
        place, stiff_ref, u_ref, far, near, ends_ref, old_ref, inv_ref, *refs = refs
    if step < SUBSTEPS - 1:
        g_ref, send_ref, vw_ref, adv_ref, pad, rhs = refs
    else:
        g_ref, send_ref, vw_ref, pad, rhs = refs
        adv_ref = None
    own = place[0]
    odd = place[1] > 0
    stiff = stiff_ref[0]

    for c in range(3):
        for x in range(2):
            pad[c, x, 8 : 8 + CY, :] = u_ref[c, x]
            if step == 0:
                odd_y = lax.rem(own, 2) > 0
                pad[c, x, 6:8, :] = jnp.where(odd_y, pair_y[c, x, 14:16, :], other_y[c, x, 14:16, :])
                pad[c, x, 8 + CY : 10 + CY, :] = jnp.where(odd_y, other_y[c, x, 0:2, :], pair_y[c, x, 0:2, :])
            else:
                line = 2 * c + x
                pad[c, x, 6:7, :] = ends_ref[0, line : line + 1, :]
                pad[c, x, 7:8, :] = ends_ref[1, line : line + 1, :]
                pad[c, x, 8 + CY : 9 + CY, :] = ends_ref[2, line : line + 1, :]
                pad[c, x, 9 + CY : 10 + CY, :] = ends_ref[3, line : line + 1, :]

    for r in range(0, CY, CHUNK):
        rows = slice(r, r + CHUNK)
        for x in range(2):
            speed = [u_ref[d, x, rows, :] for d in range(3)]
            plus = [2.0 * courant[d] * jnp.maximum(speed[d], 0.0) for d in range(3)]
            minus = [2.0 * courant[d] * jnp.minimum(speed[d], 0.0) for d in range(3)]
            total = plus[0] - minus[0]
            for d in (1, 2):
                total = total + (plus[d] - minus[d])
            total = 0.75 * total
            for c in range(3):
                f = speed[c]
                low = [jnp.where(odd, near[c, i, rows, :], far[c, i, rows, :]) for i in range(x, 2)]
                high = [jnp.where(odd, far[c, i, rows, :], near[c, i, rows, :]) for i in range(0, x + 1)]
                line = low + [u_ref[c, 0, rows, :], u_ref[c, 1, rows, :]] + high
                at = 2 if x == 0 else 2
                b2, b1, a1, a2 = line[at - 2], line[at - 1], line[at + 1], line[at + 2]
                adv = total * f
                adv = adv + plus[0] * (0.25 * b2 - b1) + minus[0] * (a1 - 0.25 * a2)
                y2, y1 = pad[c, x, 6 + r : 6 + r + CHUNK, :], pad[c, x, 7 + r : 7 + r + CHUNK, :]
                w1, w2 = pad[c, x, 9 + r : 9 + r + CHUNK, :], pad[c, x, 10 + r : 10 + r + CHUNK, :]
                adv = adv + plus[1] * (0.25 * y2 - y1) + minus[1] * (w1 - 0.25 * w2)
                z1, z2 = pltpu.roll(f, 1, 1), pltpu.roll(f, 2, 1)
                t1, t2 = pltpu.roll(f, LANES - 1, 1), pltpu.roll(f, LANES - 2, 1)
                adv = adv + plus[2] * (0.25 * z2 - z1) + minus[2] * (t1 - 0.25 * t2)
                forcing = f + (implicit_share[step] * stiff) * (w1 - 2.0 * f + y1) - new_weight[step] * adv
                if old_ref is not None:
                    forcing = forcing - old_weight[step] * old_ref[c, x, rows, :]
                if adv_ref is not None:
                    adv_ref[c, x, rows, :] = adv
                column = (2 * c + x) * LANES
                rhs[rows, column : column + LANES] = forcing

    inverse = inv_ref[step]
    first_flag = jnp.where(own > 0, 1.0, 0.0)
    last_flag = jnp.where(own < 7, 1.0, 0.0)
    coupling = -implicit_share[step] * stiff
    vw_ref[0] = jnp.broadcast_to(inverse[:, 0:1] * (coupling * first_flag), (CY, LANES))
    vw_ref[1] = jnp.broadcast_to(inverse[:, CY - 1 : CY] * (coupling * last_flag), (CY, LANES))
    for pair in range(3):
        solved = jnp.dot(
            inverse,
            rhs[:, pair * 256 : pair * 256 + 256],
            precision=lax.Precision.HIGHEST,
            preferred_element_type=jnp.float32,
        )
        g_ref[pair, 0] = solved[:, :LANES]
        g_ref[pair, 1] = solved[:, LANES:]
    for t, row in enumerate(ENDS):
        tile = jnp.concatenate(
            [g_ref[c, x, row : row + 1, :] for c in range(3) for x in range(2)]
            + [vw_ref[0, row : row + 1, :], vw_ref[1, row : row + 1, :]],
            axis=0,
        )
        for dest in range(8):
            send_ref[dest, t] = tile


def correct_kernel(step, place, got, g_ref, vw_ref, *refs):
    if step < SUBSTEPS - 1:
        u_ref, ends_ref, heads, tails = refs
    else:
        u_ref, heads, tails = refs
        ends_ref = None
    own = place[0]
    shape = (8, LANES)

    def tip(block, t, which):
        return jnp.broadcast_to(got[block, t, 6 + which : 7 + which, :], shape)

    zero = jnp.zeros(shape, jnp.float32)
    for edge in (0, 1, 10, 11):
        heads[edge] = zero
        tails[edge] = zero
    prev_q, prev_last = zero, zero
    fronts, backs, front_qs, back_qs = [], [], [], []
    for block in range(8):
        head_v, tail_v, head_w, tail_w = tip(block, 0, 0), tip(block, 3, 0), tip(block, 0, 1), tip(block, 3, 1)
        pivot = 1.0 / (1.0 - head_v * prev_q)
        front = (got[block, 0] - head_v * prev_last) * pivot
        back = got[block, 3] - tail_v * prev_last + tail_v * prev_q * front
        front_q = head_w * pivot
        back_q = tail_w + tail_v * prev_q * front_q
        fronts.append(front)
        backs.append(back)
        front_qs.append(front_q)
        back_qs.append(back_q)
        prev_q, prev_last = back_q, back
    after = zero
    for block in range(7, -1, -1):
        head = fronts[block] - front_qs[block] * after
        heads[block + 2] = head
        tails[block + 2] = backs[block] - back_qs[block] * after
        after = head

    lower = tails[own + 1]
    upper = heads[own + 3]
    for c in range(3):
        for x in range(2):
            line = 2 * c + x
            low = lower[line : line + 1, :]
            high = upper[line : line + 1, :]
            u_ref[c, x] = g_ref[c, x] - vw_ref[0] * low - vw_ref[1] * high
    if ends_ref is not None:
        before = jnp.maximum(own - 1, 0)
        behind = jnp.minimum(own + 1, 7)
        row = got[before, 2]
        row = row - jnp.broadcast_to(got[before, 2, 6:7, :], shape) * tails[own]
        row = row - jnp.broadcast_to(got[before, 2, 7:8, :], shape) * heads[own + 2]
        ends_ref[0] = jnp.where(own > 0, row, zero)
        ends_ref[1] = lower
        ends_ref[2] = upper
        row = got[behind, 1]
        row = row - jnp.broadcast_to(got[behind, 1, 6:7, :], shape) * tails[own + 2]
        row = row - jnp.broadcast_to(got[behind, 1, 7:8, :], shape) * heads[own + 4]
        ends_ref[3] = jnp.where(own < 7, row, zero)


def f32(*shape):
    return jax.ShapeDtypeStruct(shape, jnp.float32)


def body(velocity, stiffness, block_inverse):
    gx = lax.axis_size("gx")
    gy = lax.axis_size("gy")
    place = jnp.stack([lax.axis_index("gy"), lax.axis_index("gx") % 2]).astype(jnp.int32)
    field = f32(3, 2, CY, LANES)
    current = velocity
    old = None
    for step in range(SUBSTEPS):
        far = lax.ppermute(current, "gx", swaps(gx, 1, True))
        near = lax.ppermute(current, "gx", swaps(gx, 0, True))
        if step == 0:
            ends = jnp.concatenate([velocity[:, :, 0:8, :], velocity[:, :, CY - 8 : CY, :]], axis=2)
            pair_y = lax.ppermute(ends, "gy", swaps(gy, 0, False))
            other_y = lax.ppermute(ends, "gy", swaps(gy, 1, False))
            extra = [pair_y, other_y]
            specs = [VMEM] * 2
        else:
            extra = [ends, old]
            specs = [VMEM] * 2
        outs = [field, f32(8, 4, 8, LANES), f32(2, CY, LANES)]
        if step < SUBSTEPS - 1:
            outs.append(field)
        results = pl.pallas_call(
            functools.partial(forcing_kernel, step),
            out_shape=outs,
            in_specs=[SMEM, SMEM, VMEM, VMEM, VMEM] + specs + [VMEM],
            out_specs=[VMEM] * len(outs),
            scratch_shapes=[
                pltpu.VMEM((3, 2, CY + 16, LANES), jnp.float32),
                pltpu.VMEM((CY, 6 * LANES), jnp.float32),
            ],
            name=f"forcing{step}",
        )(place, stiffness, current, far, near, *extra, block_inverse)
        solved, send, vw = results[:3]
        if step < SUBSTEPS - 1:
            old = results[3]
        got = lax.all_to_all(send.reshape(8, 32, LANES), "gy", split_axis=0, concat_axis=0)
        outs = [field]
        if step < SUBSTEPS - 1:
            outs.append(f32(4, 8, LANES))
        results = pl.pallas_call(
            functools.partial(correct_kernel, step),
            out_shape=outs,
            in_specs=[SMEM, VMEM, VMEM, VMEM],
            out_specs=[VMEM] * len(outs),
            scratch_shapes=[pltpu.VMEM((12, 8, LANES), jnp.float32)] * 2,
            name=f"correct{step}",
        )(place, got.reshape(8, 4, 8, LANES), solved, vw)
        current = results[0]
        if step < SUBSTEPS - 1:
            ends = results[1]
    return current


def solution(mesh):
    return jax.shard_map(
        body,
        mesh=mesh,
        in_specs=(P(None, "gx", "gy", None), P("gy"), P(None, "gy", None)),
        out_specs=P(None, "gx", "gy", None),
        check_vma=False,
    )
```

```python
import functools

import jax
import jax.numpy as jnp
from jax import lax
from jax.experimental import pallas as pl
from jax.experimental.pallas import tpu as pltpu
from jax.sharding import PartitionSpec as P

SUBSTEPS = 3
implicit_share = (8.0 / 15.0, 2.0 / 15.0, 1.0 / 3.0)
new_weight = (8.0 / 15.0, 5.0 / 12.0, 3.0 / 4.0)
old_weight = (0.0, -17.0 / 60.0, -5.0 / 12.0)
courant = (0.3, 0.2, 0.3)

CY = 192
LANES = 128
CHUNK = 32
ENDS = (0, 1, CY - 2, CY - 1)

VMEM = pl.BlockSpec(memory_space=pltpu.VMEM)
SMEM = pl.BlockSpec(memory_space=pltpu.SMEM)


def swaps(count, offset, closed):
    pairs = []
    for a in range(offset, count + offset - 1, 2):
        b = a + 1
        if b < count:
            pairs += [(a, b), (b, a)]
        elif closed:
            pairs += [(a, 0), (0, a)]
    return pairs


def own_kernel(step, *refs):
    if step == 0:
        place, stiff_ref, u_ref, pair_y, other_y, *refs = refs
        old_ref = None
    else:
        place, stiff_ref, u_ref, ends_ref, old_ref, *refs = refs
    if step < SUBSTEPS - 1:
        part_ref, share_ref, pad = refs
    else:
        part_ref, pad = refs
        share_ref = None
    stiff = stiff_ref[0]

    for c in range(3):
        for x in range(2):
            pad[c, x, 8 : 8 + CY, :] = u_ref[c, x]
            if step == 0:
                odd_y = lax.rem(place[0], 2) > 0
                pad[c, x, 6:8, :] = jnp.where(odd_y, pair_y[c, x, 14:16, :], other_y[c, x, 14:16, :])
                pad[c, x, 8 + CY : 10 + CY, :] = jnp.where(odd_y, other_y[c, x, 0:2, :], pair_y[c, x, 0:2, :])
            else:
                line = 2 * c + x
                pad[c, x, 6:7, :] = ends_ref[0, line : line + 1, :]
                pad[c, x, 7:8, :] = ends_ref[1, line : line + 1, :]
                pad[c, x, 8 + CY : 9 + CY, :] = ends_ref[2, line : line + 1, :]
                pad[c, x, 9 + CY : 10 + CY, :] = ends_ref[3, line : line + 1, :]

    for r in range(0, CY, CHUNK):
        rows = slice(r, r + CHUNK)
        for x in range(2):
            speed = [u_ref[d, x, rows, :] for d in range(3)]
            plus = [2.0 * courant[d] * jnp.maximum(speed[d], 0.0) for d in range(3)]
            minus = [2.0 * courant[d] * jnp.minimum(speed[d], 0.0) for d in range(3)]
            total = plus[0] - minus[0]
            for d in (1, 2):
                total = total + (plus[d] - minus[d])
            total = 0.75 * total
            for c in range(3):
                f = speed[c]
                adv = total * f
                y2, y1 = pad[c, x, 6 + r : 6 + r + CHUNK, :], pad[c, x, 7 + r : 7 + r + CHUNK, :]
                w1, w2 = pad[c, x, 9 + r : 9 + r + CHUNK, :], pad[c, x, 10 + r : 10 + r + CHUNK, :]
                adv = adv + plus[1] * (0.25 * y2 - y1) + minus[1] * (w1 - 0.25 * w2)
                z1, z2 = pltpu.roll(f, 1, 1), pltpu.roll(f, 2, 1)
                t1, t2 = pltpu.roll(f, LANES - 1, 1), pltpu.roll(f, LANES - 2, 1)
                adv = adv + plus[2] * (0.25 * z2 - z1) + minus[2] * (t1 - 0.25 * t2)
                forcing = f + (implicit_share[step] * stiff) * (w1 - 2.0 * f + y1) - new_weight[step] * adv
                if old_ref is not None:
                    forcing = forcing - old_weight[step] * old_ref[c, x, rows, :]
                part_ref[c, x, rows, :] = forcing
                if share_ref is not None:
                    share_ref[c, x, rows, :] = adv


def planes_kernel(step, *refs):
    place, stiff_ref, u_ref, far, near, part_ref, inv_ref, *refs = refs
    if step > 0:
        far_lf, old_vw, *refs = refs
    if step < SUBSTEPS - 1:
        share_ref, g_ref, send_ref, vw_ref, adv_ref, rhs = refs
    else:
        g_ref, send_ref, vw_ref, rhs = refs
        share_ref = adv_ref = None
    own = place[0]
    odd = place[1] > 0
    stiff = stiff_ref[0]

    for r in range(0, CY, CHUNK):
        rows = slice(r, r + CHUNK)
        plus = [2.0 * courant[0] * jnp.maximum(u_ref[0, x, rows, :], 0.0) for x in range(2)]
        minus = [2.0 * courant[0] * jnp.minimum(u_ref[0, x, rows, :], 0.0) for x in range(2)]
        if step > 0:
            v, w = old_vw[0, rows, :], old_vw[1, rows, :]
        for c in range(3):
            away = [far[c, x, rows, :] for x in range(2)]
            if step > 0:
                for x in range(2):
                    line = 2 * c + x
                    away[x] = away[x] - v * far_lf[0, line : line + 1, :] - w * far_lf[1, line : line + 1, :]
            close = [near[c, x, rows, :] for x in range(2)]
            low = [jnp.where(odd, close[x], away[x]) for x in range(2)]
            high = [jnp.where(odd, away[x], close[x]) for x in range(2)]
            along = low + [u_ref[c, 0, rows, :], u_ref[c, 1, rows, :]] + high
            for x in range(2):
                b2, b1, a1, a2 = along[x], along[x + 1], along[x + 3], along[x + 4]
                adv = plus[x] * (0.25 * b2 - b1) + minus[x] * (a1 - 0.25 * a2)
                column = (2 * c + x) * LANES
                rhs[rows, column : column + LANES] = part_ref[c, x, rows, :] - new_weight[step] * adv
                if adv_ref is not None:
                    adv_ref[c, x, rows, :] = share_ref[c, x, rows, :] + adv

    inverse = inv_ref[step]
    first_flag = jnp.where(own > 0, 1.0, 0.0)
    last_flag = jnp.where(own < 7, 1.0, 0.0)
    coupling = -implicit_share[step] * stiff
    vw_ref[0] = jnp.broadcast_to(inverse[:, 0:1] * (coupling * first_flag), (CY, LANES))
    vw_ref[1] = jnp.broadcast_to(inverse[:, CY - 1 : CY] * (coupling * last_flag), (CY, LANES))
    for pair in range(3):
        solved = jnp.dot(
            inverse,
            rhs[:, pair * 256 : pair * 256 + 256],
            precision=lax.Precision.HIGHEST,
            preferred_element_type=jnp.float32,
        )
        g_ref[pair, 0] = solved[:, :LANES]
        g_ref[pair, 1] = solved[:, LANES:]
    for t, row in enumerate(ENDS):
        tile = jnp.concatenate(
            [g_ref[c, x, row : row + 1, :] for c in range(3) for x in range(2)]
            + [vw_ref[0, row : row + 1, :], vw_ref[1, row : row + 1, :]],
            axis=0,
        )
        for dest in range(8):
            send_ref[dest, t] = tile


def correct_kernel(step, place, got, g_ref, vw_ref, *refs):
    if step < SUBSTEPS - 1:
        u_ref, ends_ref, lf_ref, heads, tails = refs
    else:
        u_ref, heads, tails = refs
        ends_ref = None
    own = place[0]
    shape = (8, LANES)

    def tip(block, t, which):
        return jnp.broadcast_to(got[block, t, 6 + which : 7 + which, :], shape)

    zero = jnp.zeros(shape, jnp.float32)
    for edge in (0, 1, 10, 11):
        heads[edge] = zero
        tails[edge] = zero
    prev_q, prev_last = zero, zero
    fronts, backs, front_qs, back_qs = [], [], [], []
    for block in range(8):
        head_v, tail_v, head_w, tail_w = tip(block, 0, 0), tip(block, 3, 0), tip(block, 0, 1), tip(block, 3, 1)
        pivot = 1.0 / (1.0 - head_v * prev_q)
        front = (got[block, 0] - head_v * prev_last) * pivot
        back = got[block, 3] - tail_v * prev_last + tail_v * prev_q * front
        front_q = head_w * pivot
        back_q = tail_w + tail_v * prev_q * front_q
        fronts.append(front)
        backs.append(back)
        front_qs.append(front_q)
        back_qs.append(back_q)
        prev_q, prev_last = back_q, back
    after = zero
    for block in range(7, -1, -1):
        head = fronts[block] - front_qs[block] * after
        heads[block + 2] = head
        tails[block + 2] = backs[block] - back_qs[block] * after
        after = head

    lower = tails[own + 1]
    upper = heads[own + 3]
    for c in range(3):
        for x in range(2):
            line = 2 * c + x
            low = lower[line : line + 1, :]
            high = upper[line : line + 1, :]
            u_ref[c, x] = g_ref[c, x] - vw_ref[0] * low - vw_ref[1] * high
    if ends_ref is not None:
        lf_ref[0] = lower
        lf_ref[1] = upper
        before = jnp.maximum(own - 1, 0)
        behind = jnp.minimum(own + 1, 7)
        row = got[before, 2]
        row = row - jnp.broadcast_to(got[before, 2, 6:7, :], shape) * tails[own]
        row = row - jnp.broadcast_to(got[before, 2, 7:8, :], shape) * heads[own + 2]
        ends_ref[0] = jnp.where(own > 0, row, zero)
        ends_ref[1] = lower
        ends_ref[2] = upper
        row = got[behind, 1]
        row = row - jnp.broadcast_to(got[behind, 1, 6:7, :], shape) * tails[own + 2]
        row = row - jnp.broadcast_to(got[behind, 1, 7:8, :], shape) * heads[own + 4]
        ends_ref[3] = jnp.where(own < 7, row, zero)


def f32(*shape):
    return pltpu.VMEM(shape, jnp.float32)


def local(value):
    return pltpu.with_memory_space_constraint(value, pltpu.VMEM)


def call(kernel, step, scalars, arrays, outs, scratch, name, flops):
    return pl.pallas_call(
        functools.partial(kernel, step),
        out_shape=outs,
        in_specs=[SMEM] * len(scalars) + [VMEM] * len(arrays),
        out_specs=[VMEM] * len(outs),
        scratch_shapes=scratch,
        cost_estimate=pl.CostEstimate(flops=flops, bytes_accessed=4 << 20, transcendentals=0),
        compiler_params=pltpu.CompilerParams(vmem_limit_bytes=16 << 20),
        name=f"{name}{step}",
    )(*scalars, *[local(a) for a in arrays])


def body(velocity, stiffness, block_inverse):
    gx = lax.axis_size("gx")
    gy = lax.axis_size("gy")
    place = jnp.stack([lax.axis_index("gy"), lax.axis_index("gx") % 2]).astype(jnp.int32)
    field = f32(3, 2, CY, LANES)
    scalars = [place, stiffness]
    across = swaps(gx, 1, True)
    inside = swaps(gx, 0, True)
    current = velocity
    for step in range(SUBSTEPS):
        last = step == SUBSTEPS - 1
        if step == 0:
            rows = jnp.concatenate([velocity[:, :, 0:8, :], velocity[:, :, CY - 8 : CY, :]], axis=2)
            pair_y = lax.ppermute(rows, "gy", swaps(gy, 0, False))
            other_y = lax.ppermute(rows, "gy", swaps(gy, 1, False))
            far = lax.ppermute(velocity, "gx", across)
            own_args = [current, pair_y, other_y]
            far_args = []
        else:
            far_args = [lax.ppermute(lf, "gx", across), vw]
            own_args = [current, ends, adv]
        near = lax.ppermute(current, "gx", inside)
        pad = [pltpu.VMEM((3, 2, CY + 16, LANES), jnp.float32)]
        parts = call(own_kernel, step, scalars, own_args, [field] * (1 if last else 2), pad, "own", 10**8)
        outs = [field, f32(8, 4, 8, LANES), f32(2, CY, LANES)] + [field] * (0 if last else 1)
        rhs = [pltpu.VMEM((CY, 6 * LANES), jnp.float32)]
        arrays = [current, far, near, parts[0], block_inverse] + far_args + list(parts[1:])
        g, send, vw, *advs = call(planes_kernel, step, scalars, arrays, outs, rhs, "planes", 10**9)
        if not last:
            adv = advs[0]
            far = lax.ppermute(g, "gx", across)
        got = lax.all_to_all(send.reshape(8, 32, LANES), "gy", split_axis=0, concat_axis=0)
        outs = [jax.ShapeDtypeStruct((3, 2, CY, LANES), jnp.float32)]
        if not last:
            outs = [field, f32(4, 8, LANES), f32(2, 8, LANES)]
        edge = [pltpu.VMEM((12, 8, LANES), jnp.float32)] * 2
        results = call(correct_kernel, step, [place], [got.reshape(8, 4, 8, LANES), g, vw], outs, edge, "correct", 10**8)
        current = results[0]
        if not last:
            ends, lf = results[1:]
    return current


def solution(mesh):
    return jax.shard_map(
        body,
        mesh=mesh,
        in_specs=(P(None, "gx", "gy", None), P("gy"), P(None, "gy", None)),
        out_specs=P(None, "gx", "gy", None),
        check_vma=False,
    )
```

```python
import functools

import jax
import jax.numpy as jnp
from jax import lax
from jax.experimental import pallas as pl
from jax.experimental.pallas import tpu as pltpu
from jax.sharding import PartitionSpec as P


SUBSTEPS = 3
implicit_share = (8.0 / 15.0, 2.0 / 15.0, 1.0 / 3.0)
new_weight = (8.0 / 15.0, 5.0 / 12.0, 3.0 / 4.0)
old_weight = (0.0, -17.0 / 60.0, -5.0 / 12.0)
courant = (0.3, 0.2, 0.3)

CY = 192
LANES = 128
CHUNK = 32
ENDS = (0, 1, CY - 2, CY - 1)

VMEM = pl.BlockSpec(memory_space=pltpu.VMEM)
HBM = pl.BlockSpec(memory_space=pltpu.HBM)
SMEM = pl.BlockSpec(memory_space=pltpu.SMEM)


def swaps(count, offset, closed):
    pairs = []
    for a in range(offset, count + offset - 1, 2):
        b = a + 1
        if b < count:
            pairs += [(a, b), (b, a)]
        elif closed:
            pairs += [(a, 0), (0, a)]
    return pairs


def lines():
    return [(c, x) for c in range(3) for x in range(2)]


def pack_kernel(velocity, u_ref, send_ref, top, bottom, sems):
    copies = [
        pltpu.make_async_copy(velocity.at[:, :, pl.ds(0, 8), :], top, sems.at[0]),
        pltpu.make_async_copy(velocity.at[:, :, pl.ds(CY - 8, 8), :], bottom, sems.at[1]),
        pltpu.make_async_copy(velocity, u_ref, sems.at[2]),
    ]
    for copy in copies:
        copy.start()
    copies[0].wait()
    copies[1].wait()
    for t, (source, row) in enumerate(((top, 0), (top, 1), (bottom, 6), (bottom, 7))):
        picked = [source[c, x, row : row + 1, :] for c, x in lines()]
        tile = jnp.concatenate(picked + picked[:2], axis=0)
        for dest in range(8):
            send_ref[dest, t] = tile
    copies[2].wait()


def own_kernel(step, *refs):
    if step == 0:
        stiff_ref, u_ref, got, *refs = refs
        old_ref = None
        own = lax.axis_index("gy")
        before = jnp.maximum(own - 1, 0)
        behind = jnp.minimum(own + 1, 7)
        ends = [jnp.where(own > 0, got[before, t], 0.0) for t in (2, 3)]
        ends += [jnp.where(own < 7, got[behind, t], 0.0) for t in (0, 1)]
    else:
        stiff_ref, u_ref, ends_ref, old_share, old_ref, *refs = refs
        ends = [ends_ref[t] for t in range(4)]
    if step < SUBSTEPS - 1:
        part_ref, share_ref, pad = refs
    else:
        part_ref, pad = refs
        share_ref = None
    stiff = stiff_ref[0]

    for c in range(3):
        for x in range(2):
            pad[c, x, 8 : 8 + CY, :] = u_ref[c, x]
            line = slice(2 * c + x, 2 * c + x + 1)
            pad[c, x, 6:7, :] = ends[0][line]
            pad[c, x, 7:8, :] = ends[1][line]
            pad[c, x, 8 + CY : 9 + CY, :] = ends[2][line]
            pad[c, x, 9 + CY : 10 + CY, :] = ends[3][line]

    for r in range(0, CY, CHUNK):
        rows = slice(r, r + CHUNK)
        for x in range(2):
            speed = [u_ref[d, x, rows, :] for d in range(3)]
            plus = [2.0 * courant[d] * jnp.maximum(speed[d], 0.0) for d in range(3)]
            minus = [2.0 * courant[d] * jnp.minimum(speed[d], 0.0) for d in range(3)]
            total = plus[0] - minus[0]
            for d in (1, 2):
                total = total + (plus[d] - minus[d])
            total = 0.75 * total
            for c in range(3):
                f = speed[c]
                adv = total * f
                y2, y1 = pad[c, x, 6 + r : 6 + r + CHUNK, :], pad[c, x, 7 + r : 7 + r + CHUNK, :]
                w1, w2 = pad[c, x, 9 + r : 9 + r + CHUNK, :], pad[c, x, 10 + r : 10 + r + CHUNK, :]
                adv = adv + plus[1] * (0.25 * y2 - y1) + minus[1] * (w1 - 0.25 * w2)
                z1, z2 = pltpu.roll(f, 1, 1), pltpu.roll(f, 2, 1)
                t1, t2 = pltpu.roll(f, LANES - 1, 1), pltpu.roll(f, LANES - 2, 1)
                adv = adv + plus[2] * (0.25 * z2 - z1) + minus[2] * (t1 - 0.25 * t2)
                forcing = f + (implicit_share[step] * stiff) * (w1 - 2.0 * f + y1) - new_weight[step] * adv
                if old_ref is not None:
                    old = old_share[c, x, rows, :] + old_ref[c, x, rows, :]
                    forcing = forcing - old_weight[step] * old
                part_ref[c, x, rows, :] = forcing
                if share_ref is not None:
                    share_ref[c, x, rows, :] = adv


def planes_kernel(step, *refs):
    stiff_ref, inverses, u_ref, far, near, part_ref, *refs = refs
    if step > 0:
        far_lf, old_vw, *refs = refs
    if step < SUBSTEPS - 1:
        g_ref, send_ref, vw_ref, adv_ref, rhs, inv_ref, sem = refs
    else:
        g_ref, send_ref, vw_ref, rhs, inv_ref, sem = refs
        adv_ref = None
    fetch = pltpu.make_async_copy(inverses.at[step], inv_ref, sem)
    fetch.start()
    own = lax.axis_index("gy")
    odd = lax.rem(lax.axis_index("gx"), 2) > 0
    stiff = stiff_ref[0]

    for r in range(0, CY, CHUNK):
        rows = slice(r, r + CHUNK)
        plus = [2.0 * courant[0] * jnp.maximum(u_ref[0, x, rows, :], 0.0) for x in range(2)]
        minus = [2.0 * courant[0] * jnp.minimum(u_ref[0, x, rows, :], 0.0) for x in range(2)]
        if step > 0:
            v, w = old_vw[0, rows, :], old_vw[1, rows, :]
        for c in range(3):
            away = [far[c, x, rows, :] for x in range(2)]
            if step > 0:
                for x in range(2):
                    line = 2 * c + x
                    away[x] = away[x] - v * far_lf[0, line : line + 1, :] - w * far_lf[1, line : line + 1, :]
            close = [near[c, x, rows, :] for x in range(2)]
            low = [jnp.where(odd, close[x], away[x]) for x in range(2)]
            high = [jnp.where(odd, away[x], close[x]) for x in range(2)]
            along = low + [u_ref[c, 0, rows, :], u_ref[c, 1, rows, :]] + high
            for x in range(2):
                b2, b1, a1, a2 = along[x], along[x + 1], along[x + 3], along[x + 4]
                adv = plus[x] * (0.25 * b2 - b1) + minus[x] * (a1 - 0.25 * a2)
                column = (2 * c + x) * LANES
                rhs[rows, column : column + LANES] = part_ref[c, x, rows, :] - new_weight[step] * adv
                if adv_ref is not None:
                    adv_ref[c, x, rows, :] = adv

    fetch.wait()
    inverse = inv_ref[...]
    first_flag = jnp.where(own > 0, 1.0, 0.0)
    last_flag = jnp.where(own < 7, 1.0, 0.0)
    coupling = -implicit_share[step] * stiff
    vw_ref[0] = jnp.broadcast_to(inverse[:, 0:1] * (coupling * first_flag), (CY, LANES))
    vw_ref[1] = jnp.broadcast_to(inverse[:, CY - 1 : CY] * (coupling * last_flag), (CY, LANES))
    for pair in range(3):
        solved = jnp.dot(
            inverse,
            rhs[:, pair * 256 : pair * 256 + 256],
            precision=lax.Precision.HIGHEST,
            preferred_element_type=jnp.float32,
        )
        g_ref[pair, 0] = solved[:, :LANES]
        g_ref[pair, 1] = solved[:, LANES:]
    for t, row in enumerate(ENDS):
        tile = jnp.concatenate(
            [g_ref[c, x, row : row + 1, :] for c in range(3) for x in range(2)]
            + [vw_ref[0, row : row + 1, :], vw_ref[1, row : row + 1, :]],
            axis=0,
        )
        for dest in range(8):
            send_ref[dest, t] = tile


def correct_kernel(step, got, g_ref, vw_ref, *refs):
    if step < SUBSTEPS - 1:
        u_ref, ends_ref, lf_ref, heads, tails = refs
    else:
        out_ref, heads, tails, u_ref, sems = refs
        ends_ref = None
    own = lax.axis_index("gy")
    shape = (8, LANES)

    def tip(block, t, which):
        return jnp.broadcast_to(got[block, t, 6 + which : 7 + which, :], shape)

    zero = jnp.zeros(shape, jnp.float32)
    for edge in (0, 1, 10, 11):
        heads[edge] = zero
        tails[edge] = zero
    prev_q, prev_last = zero, zero
    fronts, backs, front_qs, back_qs = [], [], [], []
    for block in range(8):
        head_v, tail_v, head_w, tail_w = tip(block, 0, 0), tip(block, 3, 0), tip(block, 0, 1), tip(block, 3, 1)
        pivot = 1.0 / (1.0 - head_v * prev_q)
        front = (got[block, 0] - head_v * prev_last) * pivot
        back = got[block, 3] - tail_v * prev_last + tail_v * prev_q * front
        front_q = head_w * pivot
        back_q = tail_w + tail_v * prev_q * front_q
        fronts.append(front)
        backs.append(back)
        front_qs.append(front_q)
        back_qs.append(back_q)
        prev_q, prev_last = back_q, back
    after = zero
    for block in range(7, -1, -1):
        head = fronts[block] - front_qs[block] * after
        heads[block + 2] = head
        tails[block + 2] = backs[block] - back_qs[block] * after
        after = head

    lower = tails[own + 1]
    upper = heads[own + 3]
    for c in range(3):
        for x in range(2):
            line = 2 * c + x
            low = lower[line : line + 1, :]
            high = upper[line : line + 1, :]
            u_ref[c, x] = g_ref[c, x] - vw_ref[0] * low - vw_ref[1] * high
        if ends_ref is None:
            pltpu.make_async_copy(u_ref.at[c], out_ref.at[c], sems.at[c]).start()
    if ends_ref is None:
        for c in range(3):
            pltpu.make_async_copy(u_ref.at[c], out_ref.at[c], sems.at[c]).wait()
    if ends_ref is not None:
        lf_ref[0] = lower
        lf_ref[1] = upper
        before = jnp.maximum(own - 1, 0)
        behind = jnp.minimum(own + 1, 7)
        row = got[before, 2]
        row = row - jnp.broadcast_to(got[before, 2, 6:7, :], shape) * tails[own]
        row = row - jnp.broadcast_to(got[before, 2, 7:8, :], shape) * heads[own + 2]
        ends_ref[0] = jnp.where(own > 0, row, zero)
        ends_ref[1] = lower
        ends_ref[2] = upper
        row = got[behind, 1]
        row = row - jnp.broadcast_to(got[behind, 1, 6:7, :], shape) * tails[own + 2]
        row = row - jnp.broadcast_to(got[behind, 1, 7:8, :], shape) * heads[own + 4]
        ends_ref[3] = jnp.where(own < 7, row, zero)


def f32(*shape):
    return pltpu.VMEM(shape, jnp.float32)


def call(kernel, arrays, outs, scratch, flops, scalars=(), large=(), out_hbm=False):
    return pl.pallas_call(
        kernel,
        out_shape=outs,
        in_specs=[SMEM] * len(scalars) + [HBM] * len(large) + [VMEM] * len(arrays),
        out_specs=[HBM if out_hbm else VMEM] * len(outs),
        scratch_shapes=scratch,
        cost_estimate=pl.CostEstimate(flops=flops, bytes_accessed=4 << 20, transcendentals=0),
        compiler_params=pltpu.CompilerParams(vmem_limit_bytes=16 << 20),
    )(
        *scalars,
        *[pltpu.with_memory_space_constraint(a, pltpu.HBM) for a in large],
        *[pltpu.with_memory_space_constraint(a, pltpu.VMEM) for a in arrays],
    )


def exchange(send):
    tiles = lax.all_to_all(send.reshape(8, 32, LANES), "gy", split_axis=0, concat_axis=0)
    return tiles.reshape(8, 4, 8, LANES)


def scratch(*shape):
    return pltpu.VMEM(shape, jnp.float32)


def body(velocity, stiffness, block_inverse):
    gx = lax.axis_size("gx")
    field = f32(3, 2, CY, LANES)
    tiles = f32(8, 4, 8, LANES)
    across = swaps(gx, 1, True)
    inside = swaps(gx, 0, True)
    for step in range(SUBSTEPS):
        last = step == SUBSTEPS - 1
        if step == 0:
            far = lax.ppermute(velocity, "gx", across)
            edge = [scratch(3, 2, 8, LANES)] * 2 + [pltpu.SemaphoreType.DMA((3,))]
            current, send = call(pack_kernel, [], [field, tiles], edge, 10**6, large=[velocity])
            got = exchange(send)
            near = lax.ppermute(current, "gx", inside)
            own_args = [current, got]
            more_args = []
        else:
            far_lf = lax.ppermute(lf, "gx", across)
            near = lax.ppermute(current, "gx", inside)
            own_args = [current, ends, share, adv]
            more_args = [far_lf, vw]
        pad = [scratch(3, 2, CY + 16, LANES)]
        own = functools.partial(own_kernel, step)
        kept = [] if last else [field]
        part, *shares = call(own, own_args, [field] + kept, pad, 10**8, [stiffness])
        outs = [field, tiles, f32(2, CY, LANES)] + [field] * (0 if last else 1)
        arrays = [current, far, near, part] + more_args
        planes = functools.partial(planes_kernel, step)
        rhs = [scratch(CY, 6 * LANES), scratch(CY, CY), pltpu.SemaphoreType.DMA]
        g, send, vw, *advs = call(planes, arrays, outs, rhs, 10**9, [stiffness], [block_inverse])
        got = exchange(send)
        if not last:
            share, adv = shares[0], advs[0]
            far = lax.ppermute(g, "gx", across)
        correct = functools.partial(correct_kernel, step)
        edge = [scratch(12, 8, LANES)] * 2
        if last:
            outs = [jax.ShapeDtypeStruct((3, 2, CY, LANES), jnp.float32)]
            edge = edge + [scratch(3, 2, CY, LANES), pltpu.SemaphoreType.DMA((3,))]
            return call(correct, [got, g, vw], outs, edge, 10**8, out_hbm=True)[0]
        outs = [field, f32(4, 8, LANES), f32(2, 8, LANES)]
        current, ends, lf = call(correct, [got, g, vw], outs, edge, 10**8)


def solution(mesh):
    return jax.shard_map(
        body,
        mesh=mesh,
        in_specs=(P(None, "gx", "gy", None), P("gy"), P(None, "gy", None)),
        out_specs=P(None, "gx", "gy", None),
        check_vma=False,
    )
```

```python
import functools

import jax
import jax.numpy as jnp
from jax import lax
from jax.experimental import pallas as pl
from jax.experimental.pallas import tpu as pltpu
from jax.sharding import PartitionSpec as P


SUBSTEPS = 3
implicit_share = (8.0 / 15.0, 2.0 / 15.0, 1.0 / 3.0)
new_weight = (8.0 / 15.0, 5.0 / 12.0, 3.0 / 4.0)
old_weight = (0.0, -17.0 / 60.0, -5.0 / 12.0)
courant = (0.3, 0.2, 0.3)

CY = 192
LANES = 128
CHUNK = 32
ENDS = (0, 1, CY - 2, CY - 1)

VMEM = pl.BlockSpec(memory_space=pltpu.VMEM)
HBM = pl.BlockSpec(memory_space=pltpu.HBM)
SMEM = pl.BlockSpec(memory_space=pltpu.SMEM)


def swaps(count, offset, closed):
    pairs = []
    for a in range(offset, count + offset - 1, 2):
        b = a + 1
        if b < count:
            pairs += [(a, b), (b, a)]
        elif closed:
            pairs += [(a, 0), (0, a)]
    return pairs


def lines():
    return [(c, x) for c in range(3) for x in range(2)]


def pack_kernel(velocity, u_ref, rows_ref, sems):
    copies = [
        pltpu.make_async_copy(velocity.at[:, :, pl.ds(0, 8), :], rows_ref.at[:, :, pl.ds(0, 8), :], sems.at[0]),
        pltpu.make_async_copy(velocity.at[:, :, pl.ds(CY - 8, 8), :], rows_ref.at[:, :, pl.ds(8, 8), :], sems.at[1]),
        pltpu.make_async_copy(velocity, u_ref, sems.at[2]),
    ]
    for copy in copies:
        copy.start()
    for copy in copies:
        copy.wait()


def own_kernel(step, *refs):
    if step == 0:
        stiff_ref, u_ref, *refs = refs
        ends_ref = old_ref = None
    else:
        stiff_ref, u_ref, ends_ref, old_share, old_ref, *refs = refs
    if step < SUBSTEPS - 1:
        part_ref, share_ref, pad = refs
    else:
        part_ref, pad = refs
        share_ref = None
    stiff = stiff_ref[0]

    for c in range(3):
        for x in range(2):
            pad[c, x, 8 : 8 + CY, :] = u_ref[c, x]
            if step == 0:
                pad[c, x, 0:8, :] = jnp.zeros((8, LANES), jnp.float32)
                pad[c, x, 8 + CY : 16 + CY, :] = jnp.zeros((8, LANES), jnp.float32)
            else:
                line = 2 * c + x
                pad[c, x, 6:7, :] = ends_ref[0, line : line + 1, :]
                pad[c, x, 7:8, :] = ends_ref[1, line : line + 1, :]
                pad[c, x, 8 + CY : 9 + CY, :] = ends_ref[2, line : line + 1, :]
                pad[c, x, 9 + CY : 10 + CY, :] = ends_ref[3, line : line + 1, :]

    for r in range(0, CY, CHUNK):
        rows = slice(r, r + CHUNK)
        for x in range(2):
            speed = [u_ref[d, x, rows, :] for d in range(3)]
            plus = [2.0 * courant[d] * jnp.maximum(speed[d], 0.0) for d in range(3)]
            minus = [2.0 * courant[d] * jnp.minimum(speed[d], 0.0) for d in range(3)]
            total = plus[0] - minus[0]
            for d in (1, 2):
                total = total + (plus[d] - minus[d])
            total = 0.75 * total
            for c in range(3):
                f = speed[c]
                adv = total * f
                y2, y1 = pad[c, x, 6 + r : 6 + r + CHUNK, :], pad[c, x, 7 + r : 7 + r + CHUNK, :]
                w1, w2 = pad[c, x, 9 + r : 9 + r + CHUNK, :], pad[c, x, 10 + r : 10 + r + CHUNK, :]
                adv = adv + plus[1] * (0.25 * y2 - y1) + minus[1] * (w1 - 0.25 * w2)
                z1, z2 = pltpu.roll(f, 1, 1), pltpu.roll(f, 2, 1)
                t1, t2 = pltpu.roll(f, LANES - 1, 1), pltpu.roll(f, LANES - 2, 1)
                adv = adv + plus[2] * (0.25 * z2 - z1) + minus[2] * (t1 - 0.25 * t2)
                forcing = f + (implicit_share[step] * stiff) * (w1 - 2.0 * f + y1) - new_weight[step] * adv
                if old_ref is not None:
                    old = old_share[c, x, rows, :] + old_ref[c, x, rows, :]
                    forcing = forcing - old_weight[step] * old
                part_ref[c, x, rows, :] = forcing
                if share_ref is not None:
                    share_ref[c, x, rows, :] = adv


def planes_kernel(step, *refs):
    stiff_ref, inverses, u_ref, far, near, part_ref, *refs = refs
    if step > 0:
        far_lf, old_vw, *refs = refs
    else:
        pair_y, other_y, *refs = refs
    if step < SUBSTEPS - 1:
        g_ref, send_ref, vw_ref, adv_ref, rhs, inv_ref, sem = refs
    else:
        g_ref, send_ref, vw_ref, rhs, inv_ref, sem = refs
        adv_ref = None
    fetch = pltpu.make_async_copy(inverses.at[step], inv_ref, sem)
    fetch.start()
    own = lax.axis_index("gy")
    odd = lax.rem(lax.axis_index("gx"), 2) > 0
    stiff = stiff_ref[0]

    for r in range(0, CY, CHUNK):
        rows = slice(r, r + CHUNK)
        plus = [2.0 * courant[0] * jnp.maximum(u_ref[0, x, rows, :], 0.0) for x in range(2)]
        minus = [2.0 * courant[0] * jnp.minimum(u_ref[0, x, rows, :], 0.0) for x in range(2)]
        if step > 0:
            v, w = old_vw[0, rows, :], old_vw[1, rows, :]
        for c in range(3):
            away = [far[c, x, rows, :] for x in range(2)]
            if step > 0:
                for x in range(2):
                    line = 2 * c + x
                    away[x] = away[x] - v * far_lf[0, line : line + 1, :] - w * far_lf[1, line : line + 1, :]
            close = [near[c, x, rows, :] for x in range(2)]
            low = [jnp.where(odd, close[x], away[x]) for x in range(2)]
            high = [jnp.where(odd, away[x], close[x]) for x in range(2)]
            along = low + [u_ref[c, 0, rows, :], u_ref[c, 1, rows, :]] + high
            for x in range(2):
                b2, b1, a1, a2 = along[x], along[x + 1], along[x + 3], along[x + 4]
                adv = plus[x] * (0.25 * b2 - b1) + minus[x] * (a1 - 0.25 * a2)
                column = (2 * c + x) * LANES
                rhs[rows, column : column + LANES] = part_ref[c, x, rows, :] - new_weight[step] * adv
                if adv_ref is not None:
                    adv_ref[c, x, rows, :] = adv

    if step == 0:
        odd_y = lax.rem(own, 2) > 0
        for c, x in lines():
            low = jnp.where(odd_y, pair_y[c, x, 8:16, :], other_y[c, x, 8:16, :])
            high = jnp.where(odd_y, other_y[c, x, 0:8, :], pair_y[c, x, 0:8, :])
            y2, y1, w1, w2 = low[6:7], low[7:8], high[0:1], high[1:2]
            for row, viscous, up, down in (
                (0, y1, 0.25 * y2 - y1, None),
                (1, None, 0.25 * y1, None),
                (CY - 2, None, None, -0.25 * w1),
                (CY - 1, w1, None, w1 - 0.25 * w2),
            ):
                speed = u_ref[1, x, row : row + 1, :]
                if up is not None:
                    adv = 2.0 * courant[1] * jnp.maximum(speed, 0.0) * up
                else:
                    adv = 2.0 * courant[1] * jnp.minimum(speed, 0.0) * down
                adv_ref[c, x, row : row + 1, :] = adv_ref[c, x, row : row + 1, :] + adv
                change = -new_weight[step] * adv
                if viscous is not None:
                    change = change + (implicit_share[step] * stiff) * viscous
                column = slice((2 * c + x) * LANES, (2 * c + x + 1) * LANES)
                rhs[row : row + 1, column] = rhs[row : row + 1, column] + change

    fetch.wait()
    inverse = inv_ref[...]
    first_flag = jnp.where(own > 0, 1.0, 0.0)
    last_flag = jnp.where(own < 7, 1.0, 0.0)
    coupling = -implicit_share[step] * stiff
    vw_ref[0] = jnp.broadcast_to(inverse[:, 0:1] * (coupling * first_flag), (CY, LANES))
    vw_ref[1] = jnp.broadcast_to(inverse[:, CY - 1 : CY] * (coupling * last_flag), (CY, LANES))
    for pair in range(3):
        solved = jnp.dot(
            inverse,
            rhs[:, pair * 256 : pair * 256 + 256],
            precision=lax.Precision.HIGHEST,
            preferred_element_type=jnp.float32,
        )
        g_ref[pair, 0] = solved[:, :LANES]
        g_ref[pair, 1] = solved[:, LANES:]
    for t, row in enumerate(ENDS):
        tile = jnp.concatenate(
            [g_ref[c, x, row : row + 1, :] for c in range(3) for x in range(2)]
            + [vw_ref[0, row : row + 1, :], vw_ref[1, row : row + 1, :]],
            axis=0,
        )
        for dest in range(send_ref.shape[0]):
            send_ref[dest, t] = tile


def correct_kernel(step, got, g_ref, vw_ref, *refs):
    if step < SUBSTEPS - 1:
        u_ref, ends_ref, lf_ref, heads, tails, far_heads, far_tails = refs
        first = jnp.where(lax.rem(lax.axis_index("gx"), 2) > 0, 0, 8)
        sets = ((first, heads, tails), (8 - first, far_heads, far_tails))
    else:
        out_ref, heads, tails, u_ref, sems = refs
        ends_ref = None
        first = 0
        sets = ((first, heads, tails),)
    own = lax.axis_index("gy")
    shape = (8, LANES)
    zero = jnp.zeros(shape, jnp.float32)

    def tip(block, t, which):
        return jnp.broadcast_to(got[first + block, t, 6 + which : 7 + which, :], shape)

    for _, head_ref, tail_ref in sets:
        for edge in (0, 1, 10, 11):
            head_ref[edge] = zero
            tail_ref[edge] = zero
    prev_q = zero
    prev_last = [zero for _ in sets]
    fronts, backs, front_qs, back_qs = [], [], [], []
    for block in range(8):
        head_v, tail_v, head_w, tail_w = tip(block, 0, 0), tip(block, 3, 0), tip(block, 0, 1), tip(block, 3, 1)
        pivot = 1.0 / (1.0 - head_v * prev_q)
        front = [(got[base + block, 0] - head_v * last) * pivot for (base, _, _), last in zip(sets, prev_last)]
        back = [
            got[base + block, 3] - tail_v * last + tail_v * prev_q * new
            for (base, _, _), last, new in zip(sets, prev_last, front)
        ]
        front_q = head_w * pivot
        back_q = tail_w + tail_v * prev_q * front_q
        fronts.append(front)
        backs.append(back)
        front_qs.append(front_q)
        back_qs.append(back_q)
        prev_q, prev_last = back_q, back
    after = [zero for _ in sets]
    for block in range(7, -1, -1):
        for n, (_, head_ref, tail_ref) in enumerate(sets):
            head_ref[block + 2] = fronts[block][n] - front_qs[block] * after[n]
            tail_ref[block + 2] = backs[block][n] - back_qs[block] * after[n]
        after = [fronts[block][n] - front_qs[block] * after[n] for n in range(len(sets))]

    lower = tails[own + 1]
    upper = heads[own + 3]
    for c in range(3):
        for x in range(2):
            line = 2 * c + x
            low = lower[line : line + 1, :]
            high = upper[line : line + 1, :]
            u_ref[c, x] = g_ref[c, x] - vw_ref[0] * low - vw_ref[1] * high
        if ends_ref is None:
            pltpu.make_async_copy(u_ref.at[c], out_ref.at[c], sems.at[c]).start()
    if ends_ref is None:
        for c in range(3):
            pltpu.make_async_copy(u_ref.at[c], out_ref.at[c], sems.at[c]).wait()
    if ends_ref is not None:
        lf_ref[0] = far_tails[own + 1]
        lf_ref[1] = far_heads[own + 3]
        before = first + jnp.maximum(own - 1, 0)
        behind = first + jnp.minimum(own + 1, 7)
        row = got[before, 2]
        row = row - jnp.broadcast_to(got[before, 2, 6:7, :], shape) * tails[own]
        row = row - jnp.broadcast_to(got[before, 2, 7:8, :], shape) * heads[own + 2]
        ends_ref[0] = jnp.where(own > 0, row, zero)
        ends_ref[1] = lower
        ends_ref[2] = upper
        row = got[behind, 1]
        row = row - jnp.broadcast_to(got[behind, 1, 6:7, :], shape) * tails[own + 2]
        row = row - jnp.broadcast_to(got[behind, 1, 7:8, :], shape) * heads[own + 4]
        ends_ref[3] = jnp.where(own < 7, row, zero)


def f32(*shape):
    return pltpu.VMEM(shape, jnp.float32)


def call(kernel, arrays, outs, scratch, flops, scalars=(), large=(), out_hbm=False):
    return pl.pallas_call(
        kernel,
        out_shape=outs,
        in_specs=[SMEM] * len(scalars) + [HBM] * len(large) + [VMEM] * len(arrays),
        out_specs=[HBM if out_hbm else VMEM] * len(outs),
        scratch_shapes=scratch,
        cost_estimate=pl.CostEstimate(flops=flops, bytes_accessed=4 << 20, transcendentals=0),
        compiler_params=pltpu.CompilerParams(vmem_limit_bytes=16 << 20),
    )(
        *scalars,
        *[pltpu.with_memory_space_constraint(a, pltpu.HBM) for a in large],
        *[pltpu.with_memory_space_constraint(a, pltpu.VMEM) for a in arrays],
    )


def exchange(send, gx, gy):
    count = send.shape[0]
    send = send.reshape(count, 32, LANES)
    if count == gy:
        tiles = lax.all_to_all(send, "gy", split_axis=0, concat_axis=0)
    else:
        groups = [[((a + side) % gx) * gy + k for side in (0, 1) for k in range(gy)] for a in range(1, gx, 2)]
        tiles = lax.all_to_all(send, ("gx", "gy"), split_axis=0, concat_axis=0, axis_index_groups=groups)
    return tiles.reshape(count, 4, 8, LANES)


def scratch(*shape):
    return pltpu.VMEM(shape, jnp.float32)


def body(velocity, stiffness, block_inverse):
    gx = lax.axis_size("gx")
    gy = lax.axis_size("gy")
    field = f32(3, 2, CY, LANES)
    across = swaps(gx, 1, True)
    inside = swaps(gx, 0, True)
    for step in range(SUBSTEPS):
        last = step == SUBSTEPS - 1
        if step == 0:
            far = lax.ppermute(velocity, "gx", across)
            outs = [field, f32(3, 2, 16, LANES)]
            current, rows = call(pack_kernel, [], outs, [pltpu.SemaphoreType.DMA((3,))], 10**6, large=[velocity])
            pair_y = lax.ppermute(rows, "gy", swaps(gy, 0, False))
            other_y = lax.ppermute(rows, "gy", swaps(gy, 1, False))
            own_args = [current]
            more_args = [pair_y, other_y]
        else:
            own_args = [current, ends, share, adv]
            more_args = [far_lf, vw]
        near = lax.ppermute(current, "gx", inside)
        pad = [scratch(3, 2, CY + 16, LANES)]
        own = functools.partial(own_kernel, step)
        part, *shares = call(own, own_args, [field] * (1 if last else 2), pad, 10**8, [stiffness])
        tiles = f32(8 if last else 16, 4, 8, LANES)
        outs = [field, tiles, f32(2, CY, LANES)] + [field] * (0 if last else 1)
        arrays = [current, far, near, part] + more_args
        planes = functools.partial(planes_kernel, step)
        rhs = [scratch(CY, 6 * LANES), scratch(CY, CY), pltpu.SemaphoreType.DMA]
        g, send, vw, *advs = call(planes, arrays, outs, rhs, 10**9, [stiffness], [block_inverse])
        got = exchange(send, gx, gy)
        if not last:
            share, adv = shares[0], advs[0]
            far = lax.ppermute(g, "gx", across)
        correct = functools.partial(correct_kernel, step)
        edge = [scratch(12, 8, LANES)] * 2
        if last:
            outs = [jax.ShapeDtypeStruct((3, 2, CY, LANES), jnp.float32)]
            edge = edge + [scratch(3, 2, CY, LANES), pltpu.SemaphoreType.DMA((3,))]
            return call(correct, [got, g, vw], outs, edge, 10**8, out_hbm=True)[0]
        outs = [field, f32(4, 8, LANES), f32(2, 8, LANES)]
        current, ends, far_lf = call(correct, [got, g, vw], outs, edge * 2, 10**8)


def solution(mesh):
    return jax.shard_map(
        body,
        mesh=mesh,
        in_specs=(P(None, "gx", "gy", None), P("gy"), P(None, "gy", None)),
        out_specs=P(None, "gx", "gy", None),
        check_vma=False,
    )
```

```python
import functools

import jax
import jax.numpy as jnp
from jax import lax
from jax.experimental import pallas as pl
from jax.experimental.pallas import tpu as pltpu
from jax.sharding import PartitionSpec as P


SUBSTEPS = 3
implicit_share = (8.0 / 15.0, 2.0 / 15.0, 1.0 / 3.0)
new_weight = (8.0 / 15.0, 5.0 / 12.0, 3.0 / 4.0)
old_weight = (0.0, -17.0 / 60.0, -5.0 / 12.0)
courant = (0.3, 0.2, 0.3)

CY = 192
LANES = 128
CHUNK = 32
ENDS = (0, 1, CY - 2, CY - 1)

VMEM = pl.BlockSpec(memory_space=pltpu.VMEM)
HBM = pl.BlockSpec(memory_space=pltpu.HBM)
SMEM = pl.BlockSpec(memory_space=pltpu.SMEM)


def swaps(count, offset, closed):
    pairs = []
    for a in range(offset, count + offset - 1, 2):
        b = a + 1
        if b < count:
            pairs += [(a, b), (b, a)]
        elif closed:
            pairs += [(a, 0), (0, a)]
    return pairs


def lines():
    return [(c, x) for c in range(3) for x in range(2)]


def pack_kernel(velocity, u_ref, rows_ref, sems):
    copies = [
        pltpu.make_async_copy(velocity.at[:, :, pl.ds(0, 8), :], rows_ref.at[:, :, pl.ds(0, 8), :], sems.at[0]),
        pltpu.make_async_copy(velocity.at[:, :, pl.ds(CY - 8, 8), :], rows_ref.at[:, :, pl.ds(8, 8), :], sems.at[1]),
        pltpu.make_async_copy(velocity, u_ref, sems.at[2]),
    ]
    for copy in copies:
        copy.start()
    for copy in copies:
        copy.wait()


def own_kernel(step, *refs):
    if step == 0:
        stiff_ref, u_ref, *refs = refs
        ends_ref = old_ref = None
    else:
        stiff_ref, u_ref, ends_ref, old_share, old_ref, *refs = refs
    if step < SUBSTEPS - 1:
        part_ref, share_ref, pad = refs
    else:
        part_ref, pad = refs
        share_ref = None
    stiff = stiff_ref[0]

    for c in range(3):
        for x in range(2):
            pad[c, x, 8 : 8 + CY, :] = u_ref[c, x]
            if step == 0:
                pad[c, x, 0:8, :] = jnp.zeros((8, LANES), jnp.float32)
                pad[c, x, 8 + CY : 16 + CY, :] = jnp.zeros((8, LANES), jnp.float32)
            else:
                line = 2 * c + x
                pad[c, x, 6:7, :] = ends_ref[0, line : line + 1, :]
                pad[c, x, 7:8, :] = ends_ref[1, line : line + 1, :]
                pad[c, x, 8 + CY : 9 + CY, :] = ends_ref[2, line : line + 1, :]
                pad[c, x, 9 + CY : 10 + CY, :] = ends_ref[3, line : line + 1, :]

    for r in range(0, CY, CHUNK):
        rows = slice(r, r + CHUNK)
        for x in range(2):
            speed = [u_ref[d, x, rows, :] for d in range(3)]
            plus = [2.0 * courant[d] * jnp.maximum(speed[d], 0.0) for d in range(3)]
            minus = [2.0 * courant[d] * jnp.minimum(speed[d], 0.0) for d in range(3)]
            total = plus[0] - minus[0]
            for d in (1, 2):
                total = total + (plus[d] - minus[d])
            total = 0.75 * total
            for c in range(3):
                f = speed[c]
                adv = total * f
                y2, y1 = pad[c, x, 6 + r : 6 + r + CHUNK, :], pad[c, x, 7 + r : 7 + r + CHUNK, :]
                w1, w2 = pad[c, x, 9 + r : 9 + r + CHUNK, :], pad[c, x, 10 + r : 10 + r + CHUNK, :]
                adv = adv + plus[1] * (0.25 * y2 - y1) + minus[1] * (w1 - 0.25 * w2)
                z1, z2 = pltpu.roll(f, 1, 1), pltpu.roll(f, 2, 1)
                t1, t2 = pltpu.roll(f, LANES - 1, 1), pltpu.roll(f, LANES - 2, 1)
                adv = adv + plus[2] * (0.25 * z2 - z1) + minus[2] * (t1 - 0.25 * t2)
                forcing = f + (implicit_share[step] * stiff) * (w1 - 2.0 * f + y1) - new_weight[step] * adv
                if old_ref is not None:
                    old = old_share[c, x, rows, :] + old_ref[c, x, rows, :]
                    forcing = forcing - old_weight[step] * old
                part_ref[c, x, rows, :] = forcing
                if share_ref is not None:
                    share_ref[c, x, rows, :] = adv


def planes_kernel(step, *refs):
    stiff_ref, inverses, u_ref, far, near, part_ref, *refs = refs
    if step > 0:
        far_lf, old_vw, *refs = refs
    else:
        pair_y, other_y, *refs = refs
    if step < SUBSTEPS - 1:
        g_ref, send_ref, vw_ref, adv_ref, rhs, inv_ref, sem = refs
    else:
        g_ref, send_ref, vw_ref, rhs, inv_ref, sem = refs
        adv_ref = None
    fetch = pltpu.make_async_copy(inverses.at[step], inv_ref, sem)
    fetch.start()
    own = lax.axis_index("gy")
    odd = lax.rem(lax.axis_index("gx"), 2) > 0
    stiff = stiff_ref[0]

    for r in range(0, CY, CHUNK):
        rows = slice(r, r + CHUNK)
        plus = [2.0 * courant[0] * jnp.maximum(u_ref[0, x, rows, :], 0.0) for x in range(2)]
        minus = [2.0 * courant[0] * jnp.minimum(u_ref[0, x, rows, :], 0.0) for x in range(2)]
        if step > 0:
            v, w = old_vw[0, rows, :], old_vw[1, rows, :]
        for c in range(3):
            away = [far[c, x, rows, :] for x in range(2)]
            if step > 0:
                for x in range(2):
                    line = 2 * c + x
                    away[x] = away[x] - v * far_lf[0, line : line + 1, :] - w * far_lf[1, line : line + 1, :]
            close = [near[c, x, rows, :] for x in range(2)]
            low = [jnp.where(odd, close[x], away[x]) for x in range(2)]
            high = [jnp.where(odd, away[x], close[x]) for x in range(2)]
            along = low + [u_ref[c, 0, rows, :], u_ref[c, 1, rows, :]] + high
            for x in range(2):
                b2, b1, a1, a2 = along[x], along[x + 1], along[x + 3], along[x + 4]
                adv = plus[x] * (0.25 * b2 - b1) + minus[x] * (a1 - 0.25 * a2)
                column = (2 * c + x) * LANES
                rhs[rows, column : column + LANES] = part_ref[c, x, rows, :] - new_weight[step] * adv
                if adv_ref is not None:
                    adv_ref[c, x, rows, :] = adv

    if step == 0:
        odd_y = lax.rem(own, 2) > 0
        for c, x in lines():
            low = jnp.where(odd_y, pair_y[c, x, 8:16, :], other_y[c, x, 8:16, :])
            high = jnp.where(odd_y, other_y[c, x, 0:8, :], pair_y[c, x, 0:8, :])
            y2, y1, w1, w2 = low[6:7], low[7:8], high[0:1], high[1:2]
            for row, viscous, up, down in (
                (0, y1, 0.25 * y2 - y1, None),
                (1, None, 0.25 * y1, None),
                (CY - 2, None, None, -0.25 * w1),
                (CY - 1, w1, None, w1 - 0.25 * w2),
            ):
                speed = u_ref[1, x, row : row + 1, :]
                if up is not None:
                    adv = 2.0 * courant[1] * jnp.maximum(speed, 0.0) * up
                else:
                    adv = 2.0 * courant[1] * jnp.minimum(speed, 0.0) * down
                adv_ref[c, x, row : row + 1, :] = adv_ref[c, x, row : row + 1, :] + adv
                change = -new_weight[step] * adv
                if viscous is not None:
                    change = change + (implicit_share[step] * stiff) * viscous
                column = slice((2 * c + x) * LANES, (2 * c + x + 1) * LANES)
                rhs[row : row + 1, column] = rhs[row : row + 1, column] + change

    fetch.wait()
    inverse = inv_ref[...]
    first_flag = jnp.where(own > 0, 1.0, 0.0)
    last_flag = jnp.where(own < 7, 1.0, 0.0)
    coupling = -implicit_share[step] * stiff
    vw_ref[0] = jnp.broadcast_to(inverse[:, 0:1] * (coupling * first_flag), (CY, LANES))
    vw_ref[1] = jnp.broadcast_to(inverse[:, CY - 1 : CY] * (coupling * last_flag), (CY, LANES))
    for pair in range(3):
        solved = jnp.dot(
            inverse,
            rhs[:, pair * 256 : pair * 256 + 256],
            precision=lax.Precision.HIGHEST,
            preferred_element_type=jnp.float32,
        )
        g_ref[pair, 0] = solved[:, :LANES]
        g_ref[pair, 1] = solved[:, LANES:]
    for t, row in enumerate(ENDS):
        tile = jnp.concatenate(
            [g_ref[c, x, row : row + 1, :] for c in range(3) for x in range(2)]
            + [vw_ref[0, row : row + 1, :], vw_ref[1, row : row + 1, :]],
            axis=0,
        )
        for dest in range(send_ref.shape[0]):
            send_ref[dest, t] = tile


def correct_kernel(step, got, g_ref, vw_ref, *refs):
    if step < SUBSTEPS - 1:
        u_ref, ends_ref, lf_ref, heads, tails = refs
    else:
        out_ref, heads, tails, u_ref, sems = refs
        ends_ref = None
    own = lax.axis_index("gy")
    shape = (8, LANES)
    zero = jnp.zeros(shape, jnp.float32)

    def tip(block, t, which):
        return jnp.broadcast_to(got[block, t, 6 + which : 7 + which, :], shape)

    for edge in (0, 1, 10, 11):
        heads[edge] = zero
        tails[edge] = zero
    prev_q, prev_last = zero, zero
    fronts, backs, front_qs, back_qs = [], [], [], []
    for block in range(8):
        head_v, tail_v, head_w, tail_w = tip(block, 0, 0), tip(block, 3, 0), tip(block, 0, 1), tip(block, 3, 1)
        pivot = 1.0 / (1.0 - head_v * prev_q)
        front = (got[block, 0] - head_v * prev_last) * pivot
        back = got[block, 3] - tail_v * prev_last + tail_v * prev_q * front
        front_q = head_w * pivot
        back_q = tail_w + tail_v * prev_q * front_q
        fronts.append(front)
        backs.append(back)
        front_qs.append(front_q)
        back_qs.append(back_q)
        prev_q, prev_last = back_q, back
    after = zero
    for block in range(7, -1, -1):
        head = fronts[block] - front_qs[block] * after
        heads[block + 2] = head
        tails[block + 2] = backs[block] - back_qs[block] * after
        after = head

    lower = tails[own + 1]
    upper = heads[own + 3]
    for c in range(3):
        for x in range(2):
            line = 2 * c + x
            low = lower[line : line + 1, :]
            high = upper[line : line + 1, :]
            u_ref[c, x] = g_ref[c, x] - vw_ref[0] * low - vw_ref[1] * high
        if ends_ref is None:
            pltpu.make_async_copy(u_ref.at[c], out_ref.at[c], sems.at[c]).start()
    if ends_ref is None:
        for c in range(3):
            pltpu.make_async_copy(u_ref.at[c], out_ref.at[c], sems.at[c]).wait()
    if ends_ref is not None:
        lf_ref[0] = lower
        lf_ref[1] = upper
        before = jnp.maximum(own - 1, 0)
        behind = jnp.minimum(own + 1, 7)
        row = got[before, 2]
        row = row - jnp.broadcast_to(got[before, 2, 6:7, :], shape) * tails[own]
        row = row - jnp.broadcast_to(got[before, 2, 7:8, :], shape) * heads[own + 2]
        ends_ref[0] = jnp.where(own > 0, row, zero)
        ends_ref[1] = lower
        ends_ref[2] = upper
        row = got[behind, 1]
        row = row - jnp.broadcast_to(got[behind, 1, 6:7, :], shape) * tails[own + 2]
        row = row - jnp.broadcast_to(got[behind, 1, 7:8, :], shape) * heads[own + 4]
        ends_ref[3] = jnp.where(own < 7, row, zero)


def f32(*shape):
    return pltpu.VMEM(shape, jnp.float32)


def call(kernel, arrays, outs, scratch, flops, scalars=(), large=(), out_hbm=False):
    return pl.pallas_call(
        kernel,
        out_shape=outs,
        in_specs=[SMEM] * len(scalars) + [HBM] * len(large) + [VMEM] * len(arrays),
        out_specs=[HBM if out_hbm else VMEM] * len(outs),
        scratch_shapes=scratch,
        cost_estimate=pl.CostEstimate(flops=flops, bytes_accessed=4 << 20, transcendentals=0),
        compiler_params=pltpu.CompilerParams(vmem_limit_bytes=16 << 20),
    )(
        *scalars,
        *[pltpu.with_memory_space_constraint(a, pltpu.HBM) for a in large],
        *[pltpu.with_memory_space_constraint(a, pltpu.VMEM) for a in arrays],
    )


def exchange(send):
    tiles = lax.all_to_all(send.reshape(8, 32, LANES), "gy", split_axis=0, concat_axis=0)
    return tiles.reshape(8, 4, 8, LANES)


def scratch(*shape):
    return pltpu.VMEM(shape, jnp.float32)


def body(velocity, stiffness, block_inverse):
    gx = lax.axis_size("gx")
    gy = lax.axis_size("gy")
    field = f32(3, 2, CY, LANES)
    across = swaps(gx, 1, True)
    inside = swaps(gx, 0, True)
    for step in range(SUBSTEPS):
        last = step == SUBSTEPS - 1
        if step == 0:
            far = lax.ppermute(velocity, "gx", across)
            outs = [field, f32(3, 2, 16, LANES)]
            current, rows = call(pack_kernel, [], outs, [pltpu.SemaphoreType.DMA((3,))], 10**6, large=[velocity])
            pair_y = lax.ppermute(rows, "gy", swaps(gy, 0, False))
            other_y = lax.ppermute(rows, "gy", swaps(gy, 1, False))
            own_args = [current]
            more_args = [pair_y, other_y]
        else:
            far_lf = lax.ppermute(lf, "gx", across)
            own_args = [current, ends, share, adv]
            more_args = [far_lf, vw]
        near = lax.ppermute(current, "gx", inside)
        pad = [scratch(3, 2, CY + 16, LANES)]
        own = functools.partial(own_kernel, step)
        part, *shares = call(own, own_args, [field] * (1 if last else 2), pad, 10**8, [stiffness])
        tiles = f32(8, 4, 8, LANES)
        outs = [field, tiles, f32(2, CY, LANES)] + [field] * (0 if last else 1)
        arrays = [current, far, near, part] + more_args
        planes = functools.partial(planes_kernel, step)
        rhs = [scratch(CY, 6 * LANES), scratch(CY, CY), pltpu.SemaphoreType.DMA]
        g, send, vw, *advs = call(planes, arrays, outs, rhs, 10**9, [stiffness], [block_inverse])
        got = exchange(send)
        if not last:
            share, adv = shares[0], advs[0]
            far = lax.ppermute(g, "gx", across)
        correct = functools.partial(correct_kernel, step)
        edge = [scratch(12, 8, LANES)] * 2
        if last:
            outs = [jax.ShapeDtypeStruct((3, 2, CY, LANES), jnp.float32)]
            edge = edge + [scratch(3, 2, CY, LANES), pltpu.SemaphoreType.DMA((3,))]
            return call(correct, [got, g, vw], outs, edge, 10**8, out_hbm=True)[0]
        outs = [field, f32(4, 8, LANES), f32(2, 8, LANES)]
        current, ends, lf = call(correct, [got, g, vw], outs, edge, 10**8)


def solution(mesh):
    return jax.shard_map(
        body,
        mesh=mesh,
        in_specs=(P(None, "gx", "gy", None), P("gy"), P(None, "gy", None)),
        out_specs=P(None, "gx", "gy", None),
        check_vma=False,
    )
```

```python
import functools

import jax
import jax.numpy as jnp
from jax import lax
from jax.experimental import pallas as pl
from jax.experimental.pallas import tpu as pltpu
from jax.sharding import PartitionSpec as P


SUBSTEPS = 3
implicit_share = (8.0 / 15.0, 2.0 / 15.0, 1.0 / 3.0)
new_weight = (8.0 / 15.0, 5.0 / 12.0, 3.0 / 4.0)
old_weight = (0.0, -17.0 / 60.0, -5.0 / 12.0)
courant = (0.3, 0.2, 0.3)

CY = 192
LANES = 128
CHUNK = 32
ENDS = (0, 1, CY - 2, CY - 1)

VMEM = pl.BlockSpec(memory_space=pltpu.VMEM)
HBM = pl.BlockSpec(memory_space=pltpu.HBM)
SMEM = pl.BlockSpec(memory_space=pltpu.SMEM)


def swaps(count, offset, closed):
    pairs = []
    for a in range(offset, count + offset - 1, 2):
        b = a + 1
        if b < count:
            pairs += [(a, b), (b, a)]
        elif closed:
            pairs += [(a, 0), (0, a)]
    return pairs


def lines():
    return [(c, x) for c in range(3) for x in range(2)]


def pack_kernel(velocity, u_ref, rows_ref, sems):
    copies = [
        pltpu.make_async_copy(velocity.at[:, :, pl.ds(0, 8), :], rows_ref.at[:, :, pl.ds(0, 8), :], sems.at[0]),
        pltpu.make_async_copy(velocity.at[:, :, pl.ds(CY - 8, 8), :], rows_ref.at[:, :, pl.ds(8, 8), :], sems.at[1]),
        pltpu.make_async_copy(velocity, u_ref, sems.at[2]),
    ]
    for copy in copies:
        copy.start()
    for copy in copies:
        copy.wait()


def own_kernel(step, *refs):
    if step == 0:
        stiff_ref, u_ref, *refs = refs
        ends_ref = old_ref = None
    else:
        stiff_ref, u_ref, ends_ref, old_share, old_ref, *refs = refs
    if step < SUBSTEPS - 1:
        part_ref, share_ref, pad = refs
    else:
        part_ref, pad = refs
        share_ref = None
    stiff = stiff_ref[0]

    for c in range(3):
        for x in range(2):
            pad[c, x, 8 : 8 + CY, :] = u_ref[c, x]
            if step == 0:
                pad[c, x, 0:8, :] = jnp.zeros((8, LANES), jnp.float32)
                pad[c, x, 8 + CY : 16 + CY, :] = jnp.zeros((8, LANES), jnp.float32)
            else:
                line = 2 * c + x
                pad[c, x, 6:7, :] = ends_ref[0, line : line + 1, :]
                pad[c, x, 7:8, :] = ends_ref[1, line : line + 1, :]
                pad[c, x, 8 + CY : 9 + CY, :] = ends_ref[2, line : line + 1, :]
                pad[c, x, 9 + CY : 10 + CY, :] = ends_ref[3, line : line + 1, :]

    for r in range(0, CY, CHUNK):
        rows = slice(r, r + CHUNK)
        for x in range(2):
            speed = [u_ref[d, x, rows, :] for d in range(3)]
            plus = [2.0 * courant[d] * jnp.maximum(speed[d], 0.0) for d in range(3)]
            minus = [2.0 * courant[d] * jnp.minimum(speed[d], 0.0) for d in range(3)]
            total = plus[0] - minus[0]
            for d in (1, 2):
                total = total + (plus[d] - minus[d])
            total = 0.75 * total
            for c in range(3):
                f = speed[c]
                adv = total * f
                y2, y1 = pad[c, x, 6 + r : 6 + r + CHUNK, :], pad[c, x, 7 + r : 7 + r + CHUNK, :]
                w1, w2 = pad[c, x, 9 + r : 9 + r + CHUNK, :], pad[c, x, 10 + r : 10 + r + CHUNK, :]
                adv = adv + plus[1] * (0.25 * y2 - y1) + minus[1] * (w1 - 0.25 * w2)
                z1, z2 = pltpu.roll(f, 1, 1), pltpu.roll(f, 2, 1)
                t1, t2 = pltpu.roll(f, LANES - 1, 1), pltpu.roll(f, LANES - 2, 1)
                adv = adv + plus[2] * (0.25 * z2 - z1) + minus[2] * (t1 - 0.25 * t2)
                forcing = f + (implicit_share[step] * stiff) * (w1 - 2.0 * f + y1) - new_weight[step] * adv
                if old_ref is not None:
                    old = old_share[c, x, rows, :] + old_ref[c, x, rows, :]
                    forcing = forcing - old_weight[step] * old
                part_ref[c, x, rows, :] = forcing
                if share_ref is not None:
                    share_ref[c, x, rows, :] = adv


def planes_kernel(step, *refs):
    stiff_ref, inverses, u_ref, far, near, part_ref, *refs = refs
    if step > 0:
        far_lf, near_lf, old_vw, *refs = refs
    else:
        pair_y, other_y, *refs = refs
    if step < SUBSTEPS - 1:
        g_ref, send_ref, vw_ref, adv_ref, rhs, inv_ref, sem = refs
    else:
        g_ref, send_ref, vw_ref, rhs, inv_ref, sem = refs
        adv_ref = None
    fetch = pltpu.make_async_copy(inverses.at[step], inv_ref, sem)
    fetch.start()
    own = lax.axis_index("gy")
    odd = lax.rem(lax.axis_index("gx"), 2) > 0
    stiff = stiff_ref[0]

    for r in range(0, CY, CHUNK):
        rows = slice(r, r + CHUNK)
        plus = [2.0 * courant[0] * jnp.maximum(u_ref[0, x, rows, :], 0.0) for x in range(2)]
        minus = [2.0 * courant[0] * jnp.minimum(u_ref[0, x, rows, :], 0.0) for x in range(2)]
        if step > 0:
            v, w = old_vw[0, rows, :], old_vw[1, rows, :]
        for c in range(3):
            away = [far[c, x, rows, :] for x in range(2)]
            close = [near[c, x, rows, :] for x in range(2)]
            if step > 0:
                for x in range(2):
                    line = 2 * c + x
                    away[x] = away[x] - v * far_lf[0, line : line + 1, :] - w * far_lf[1, line : line + 1, :]
                    close[x] = close[x] - v * near_lf[0, line : line + 1, :] - w * near_lf[1, line : line + 1, :]
            low = [jnp.where(odd, close[x], away[x]) for x in range(2)]
            high = [jnp.where(odd, away[x], close[x]) for x in range(2)]
            along = low + [u_ref[c, 0, rows, :], u_ref[c, 1, rows, :]] + high
            for x in range(2):
                b2, b1, a1, a2 = along[x], along[x + 1], along[x + 3], along[x + 4]
                adv = plus[x] * (0.25 * b2 - b1) + minus[x] * (a1 - 0.25 * a2)
                column = (2 * c + x) * LANES
                rhs[rows, column : column + LANES] = part_ref[c, x, rows, :] - new_weight[step] * adv
                if adv_ref is not None:
                    adv_ref[c, x, rows, :] = adv

    if step == 0:
        odd_y = lax.rem(own, 2) > 0
        for c, x in lines():
            low = jnp.where(odd_y, pair_y[c, x, 8:16, :], other_y[c, x, 8:16, :])
            high = jnp.where(odd_y, other_y[c, x, 0:8, :], pair_y[c, x, 0:8, :])
            y2, y1, w1, w2 = low[6:7], low[7:8], high[0:1], high[1:2]
            for row, viscous, up, down in (
                (0, y1, 0.25 * y2 - y1, None),
                (1, None, 0.25 * y1, None),
                (CY - 2, None, None, -0.25 * w1),
                (CY - 1, w1, None, w1 - 0.25 * w2),
            ):
                speed = u_ref[1, x, row : row + 1, :]
                if up is not None:
                    adv = 2.0 * courant[1] * jnp.maximum(speed, 0.0) * up
                else:
                    adv = 2.0 * courant[1] * jnp.minimum(speed, 0.0) * down
                adv_ref[c, x, row : row + 1, :] = adv_ref[c, x, row : row + 1, :] + adv
                change = -new_weight[step] * adv
                if viscous is not None:
                    change = change + (implicit_share[step] * stiff) * viscous
                column = slice((2 * c + x) * LANES, (2 * c + x + 1) * LANES)
                rhs[row : row + 1, column] = rhs[row : row + 1, column] + change

    fetch.wait()
    inverse = inv_ref[...]
    first_flag = jnp.where(own > 0, 1.0, 0.0)
    last_flag = jnp.where(own < 7, 1.0, 0.0)
    coupling = -implicit_share[step] * stiff
    vw_ref[0] = jnp.broadcast_to(inverse[:, 0:1] * (coupling * first_flag), (CY, LANES))
    vw_ref[1] = jnp.broadcast_to(inverse[:, CY - 1 : CY] * (coupling * last_flag), (CY, LANES))
    for pair in range(3):
        solved = jnp.dot(
            inverse,
            rhs[:, pair * 256 : pair * 256 + 256],
            precision=lax.Precision.HIGHEST,
            preferred_element_type=jnp.float32,
        )
        g_ref[pair, 0] = solved[:, :LANES]
        g_ref[pair, 1] = solved[:, LANES:]
    for t, row in enumerate(ENDS):
        tile = jnp.concatenate(
            [g_ref[c, x, row : row + 1, :] for c in range(3) for x in range(2)]
            + [vw_ref[0, row : row + 1, :], vw_ref[1, row : row + 1, :]],
            axis=0,
        )
        for dest in range(send_ref.shape[0]):
            send_ref[dest, t] = tile


def correct_kernel(step, got, g_ref, vw_ref, *refs):
    if step < SUBSTEPS - 1:
        u_ref, ends_ref, lf_ref, near_lf, heads, tails, near_heads, near_tails = refs
        first = jnp.where(lax.rem(lax.axis_index("gx"), 2) > 0, 8, 0)
        sets = ((first, heads, tails), (8 - first, near_heads, near_tails))
    else:
        out_ref, heads, tails, u_ref, sems = refs
        ends_ref = None
        first = 0
        sets = ((first, heads, tails),)
    own = lax.axis_index("gy")
    shape = (8, LANES)
    zero = jnp.zeros(shape, jnp.float32)

    def tip(block, t, which):
        return jnp.broadcast_to(got[first + block, t, 6 + which : 7 + which, :], shape)

    for _, head_ref, tail_ref in sets:
        for edge in (0, 1, 10, 11):
            head_ref[edge] = zero
            tail_ref[edge] = zero
    prev_q = zero
    prev_last = [zero for _ in sets]
    fronts, backs, front_qs, back_qs = [], [], [], []
    for block in range(8):
        head_v, tail_v, head_w, tail_w = tip(block, 0, 0), tip(block, 3, 0), tip(block, 0, 1), tip(block, 3, 1)
        pivot = 1.0 / (1.0 - head_v * prev_q)
        front = [(got[base + block, 0] - head_v * last) * pivot for (base, _, _), last in zip(sets, prev_last)]
        back = [
            got[base + block, 3] - tail_v * last + tail_v * prev_q * new
            for (base, _, _), last, new in zip(sets, prev_last, front)
        ]
        front_q = head_w * pivot
        back_q = tail_w + tail_v * prev_q * front_q
        fronts.append(front)
        backs.append(back)
        front_qs.append(front_q)
        back_qs.append(back_q)
        prev_q, prev_last = back_q, back
    after = [zero for _ in sets]
    for block in range(7, -1, -1):
        for n, (_, head_ref, tail_ref) in enumerate(sets):
            head_ref[block + 2] = fronts[block][n] - front_qs[block] * after[n]
            tail_ref[block + 2] = backs[block][n] - back_qs[block] * after[n]
        after = [fronts[block][n] - front_qs[block] * after[n] for n in range(len(sets))]

    lower = tails[own + 1]
    upper = heads[own + 3]
    for c in range(3):
        for x in range(2):
            line = 2 * c + x
            low = lower[line : line + 1, :]
            high = upper[line : line + 1, :]
            u_ref[c, x] = g_ref[c, x] - vw_ref[0] * low - vw_ref[1] * high
        if ends_ref is None:
            pltpu.make_async_copy(u_ref.at[c], out_ref.at[c], sems.at[c]).start()
    if ends_ref is None:
        for c in range(3):
            pltpu.make_async_copy(u_ref.at[c], out_ref.at[c], sems.at[c]).wait()
    if ends_ref is not None:
        lf_ref[0] = lower
        lf_ref[1] = upper
        near_lf[0] = near_tails[own + 1]
        near_lf[1] = near_heads[own + 3]
        before = first + jnp.maximum(own - 1, 0)
        behind = first + jnp.minimum(own + 1, 7)
        row = got[before, 2]
        row = row - jnp.broadcast_to(got[before, 2, 6:7, :], shape) * tails[own]
        row = row - jnp.broadcast_to(got[before, 2, 7:8, :], shape) * heads[own + 2]
        ends_ref[0] = jnp.where(own > 0, row, zero)
        ends_ref[1] = lower
        ends_ref[2] = upper
        row = got[behind, 1]
        row = row - jnp.broadcast_to(got[behind, 1, 6:7, :], shape) * tails[own + 2]
        row = row - jnp.broadcast_to(got[behind, 1, 7:8, :], shape) * heads[own + 4]
        ends_ref[3] = jnp.where(own < 7, row, zero)


def f32(*shape):
    return pltpu.VMEM(shape, jnp.float32)


def call(kernel, arrays, outs, scratch, flops, scalars=(), large=(), out_hbm=False):
    return pl.pallas_call(
        kernel,
        out_shape=outs,
        in_specs=[SMEM] * len(scalars) + [HBM] * len(large) + [VMEM] * len(arrays),
        out_specs=[HBM if out_hbm else VMEM] * len(outs),
        scratch_shapes=scratch,
        cost_estimate=pl.CostEstimate(flops=flops, bytes_accessed=4 << 20, transcendentals=0),
        compiler_params=pltpu.CompilerParams(vmem_limit_bytes=16 << 20),
    )(
        *scalars,
        *[pltpu.with_memory_space_constraint(a, pltpu.HBM) for a in large],
        *[pltpu.with_memory_space_constraint(a, pltpu.VMEM) for a in arrays],
    )


def exchange(send, gx, gy):
    count = send.shape[0]
    send = send.reshape(count, 32, LANES)
    if count == gy:
        tiles = lax.all_to_all(send, "gy", split_axis=0, concat_axis=0)
    else:
        groups = [[a * gy + k for k in range(2 * gy)] for a in range(0, gx, 2)]
        tiles = lax.all_to_all(send, ("gx", "gy"), split_axis=0, concat_axis=0, axis_index_groups=groups)
    return tiles.reshape(count, 4, 8, LANES)


def scratch(*shape):
    return pltpu.VMEM(shape, jnp.float32)


def body(velocity, stiffness, block_inverse):
    gx = lax.axis_size("gx")
    gy = lax.axis_size("gy")
    field = f32(3, 2, CY, LANES)
    across = swaps(gx, 1, True)
    inside = swaps(gx, 0, True)
    for step in range(SUBSTEPS):
        last = step == SUBSTEPS - 1
        if step == 0:
            far = lax.ppermute(velocity, "gx", across)
            outs = [field, f32(3, 2, 16, LANES)]
            current, rows = call(pack_kernel, [], outs, [pltpu.SemaphoreType.DMA((3,))], 10**6, large=[velocity])
            pair_y = lax.ppermute(rows, "gy", swaps(gy, 0, False))
            other_y = lax.ppermute(rows, "gy", swaps(gy, 1, False))
            near = lax.ppermute(current, "gx", inside)
            own_args = [current]
            more_args = [pair_y, other_y]
        else:
            far_lf = lax.ppermute(lf, "gx", across)
            own_args = [current, ends, share, adv]
            more_args = [far_lf, near_lf, vw]
        pad = [scratch(3, 2, CY + 16, LANES)]
        own = functools.partial(own_kernel, step)
        part, *shares = call(own, own_args, [field] * (1 if last else 2), pad, 10**8, [stiffness])
        tiles = f32(8 if last else 16, 4, 8, LANES)
        outs = [field, tiles, f32(2, CY, LANES)] + [field] * (0 if last else 1)
        arrays = [current, far, near, part] + more_args
        planes = functools.partial(planes_kernel, step)
        rhs = [scratch(CY, 6 * LANES), scratch(CY, CY), pltpu.SemaphoreType.DMA]
        g, send, vw, *advs = call(planes, arrays, outs, rhs, 10**9, [stiffness], [block_inverse])
        got = exchange(send, gx, gy)
        if not last:
            share, adv = shares[0], advs[0]
            far = lax.ppermute(g, "gx", across)
            near = lax.ppermute(g, "gx", inside)
        correct = functools.partial(correct_kernel, step)
        edge = [scratch(12, 8, LANES)] * 2
        if last:
            outs = [jax.ShapeDtypeStruct((3, 2, CY, LANES), jnp.float32)]
            edge = edge + [scratch(3, 2, CY, LANES), pltpu.SemaphoreType.DMA((3,))]
            return call(correct, [got, g, vw], outs, edge, 10**8, out_hbm=True)[0]
        outs = [field, f32(4, 8, LANES), f32(2, 8, LANES), f32(2, 8, LANES)]
        current, ends, lf, near_lf = call(correct, [got, g, vw], outs, edge * 2, 10**8)


def solution(mesh):
    return jax.shard_map(
        body,
        mesh=mesh,
        in_specs=(P(None, "gx", "gy", None), P("gy"), P(None, "gy", None)),
        out_specs=P(None, "gx", "gy", None),
        check_vma=False,
    )
```

```python
import functools

import jax
import jax.numpy as jnp
from jax import lax
from jax.experimental import pallas as pl
from jax.experimental.pallas import tpu as pltpu
from jax.sharding import PartitionSpec as P


SUBSTEPS = 3
implicit_share = (8.0 / 15.0, 2.0 / 15.0, 1.0 / 3.0)
new_weight = (8.0 / 15.0, 5.0 / 12.0, 3.0 / 4.0)
old_weight = (0.0, -17.0 / 60.0, -5.0 / 12.0)
courant = (0.3, 0.2, 0.3)

CY = 192
LANES = 128
CHUNK = 32

VMEM = pl.BlockSpec(memory_space=pltpu.VMEM)
HBM = pl.BlockSpec(memory_space=pltpu.HBM)
SMEM = pl.BlockSpec(memory_space=pltpu.SMEM)


def swaps(count, offset, closed):
    pairs = []
    for a in range(offset, count + offset - 1, 2):
        b = a + 1
        if b < count:
            pairs += [(a, b), (b, a)]
        elif closed:
            pairs += [(a, 0), (0, a)]
    return pairs


def lines():
    return [(c, x) for c in range(3) for x in range(2)]


def pack_kernel(velocity, u_ref, rows_ref, sems):
    copies = [
        pltpu.make_async_copy(velocity.at[:, :, pl.ds(0, 8), :], rows_ref.at[:, :, pl.ds(0, 8), :], sems.at[0]),
        pltpu.make_async_copy(velocity.at[:, :, pl.ds(CY - 8, 8), :], rows_ref.at[:, :, pl.ds(8, 8), :], sems.at[1]),
        pltpu.make_async_copy(velocity, u_ref, sems.at[2]),
    ]
    for copy in copies:
        copy.start()
    for copy in copies:
        copy.wait()


def own_kernel(step, *refs):
    if step == 0:
        stiff_ref, inverses, u_ref, *refs = refs
        ends_ref = old_ref = None
    else:
        stiff_ref, inverses, u_ref, ends_ref, old_share, old_ref, *refs = refs
    if step < SUBSTEPS - 1:
        part_ref, inv_ref, share_ref, pad, sem = refs
    else:
        part_ref, inv_ref, pad, sem = refs
        share_ref = None
    fetch = pltpu.make_async_copy(inverses.at[step], inv_ref, sem)
    fetch.start()
    stiff = stiff_ref[0]

    for c in range(3):
        for x in range(2):
            pad[c, x, 8 : 8 + CY, :] = u_ref[c, x]
            if step == 0:
                pad[c, x, 0:8, :] = jnp.zeros((8, LANES), jnp.float32)
                pad[c, x, 8 + CY : 16 + CY, :] = jnp.zeros((8, LANES), jnp.float32)
            else:
                line = 2 * c + x
                pad[c, x, 6:7, :] = ends_ref[0, line : line + 1, :]
                pad[c, x, 7:8, :] = ends_ref[1, line : line + 1, :]
                pad[c, x, 8 + CY : 9 + CY, :] = ends_ref[2, line : line + 1, :]
                pad[c, x, 9 + CY : 10 + CY, :] = ends_ref[3, line : line + 1, :]

    for r in range(0, CY, CHUNK):
        rows = slice(r, r + CHUNK)
        for x in range(2):
            speed = [u_ref[d, x, rows, :] for d in range(3)]
            plus = [2.0 * courant[d] * jnp.maximum(speed[d], 0.0) for d in range(3)]
            minus = [2.0 * courant[d] * jnp.minimum(speed[d], 0.0) for d in range(3)]
            total = plus[0] - minus[0]
            for d in (1, 2):
                total = total + (plus[d] - minus[d])
            total = 0.75 * total
            for c in range(3):
                f = speed[c]
                adv = total * f
                y2, y1 = pad[c, x, 6 + r : 6 + r + CHUNK, :], pad[c, x, 7 + r : 7 + r + CHUNK, :]
                w1, w2 = pad[c, x, 9 + r : 9 + r + CHUNK, :], pad[c, x, 10 + r : 10 + r + CHUNK, :]
                adv = adv + plus[1] * (0.25 * y2 - y1) + minus[1] * (w1 - 0.25 * w2)
                z1, z2 = pltpu.roll(f, 1, 1), pltpu.roll(f, 2, 1)
                t1, t2 = pltpu.roll(f, LANES - 1, 1), pltpu.roll(f, LANES - 2, 1)
                adv = adv + plus[2] * (0.25 * z2 - z1) + minus[2] * (t1 - 0.25 * t2)
                forcing = f + (implicit_share[step] * stiff) * (w1 - 2.0 * f + y1) - new_weight[step] * adv
                if old_ref is not None:
                    old = old_share[c, x, rows, :] + old_ref[c, x, rows, :]
                    forcing = forcing - old_weight[step] * old
                part_ref[c, x, rows, :] = forcing
                if share_ref is not None:
                    share_ref[c, x, rows, :] = adv
    fetch.wait()


def planes_kernel(step, *refs):
    stiff_ref, u_ref, far, near, part_ref, inv_ref, *refs = refs
    if step > 0:
        far_lf, old_vw, *refs = refs
    else:
        pair_y, other_y, *refs = refs
    if step < SUBSTEPS - 1:
        g_ref, vw_ref, adv_ref, send_ref, rhs, packed, sems = refs
    else:
        g_ref, vw_ref, send_ref, rhs = refs
        adv_ref = None
    own = lax.axis_index("gy")
    odd = lax.rem(lax.axis_index("gx"), 2) > 0
    stiff = stiff_ref[0]

    for r in range(0, CY, CHUNK):
        rows = slice(r, r + CHUNK)
        plus = [2.0 * courant[0] * jnp.maximum(u_ref[0, x, rows, :], 0.0) for x in range(2)]
        minus = [2.0 * courant[0] * jnp.minimum(u_ref[0, x, rows, :], 0.0) for x in range(2)]
        if step > 0:
            v, w = old_vw[0, rows, :], old_vw[1, rows, :]
        for c in range(3):
            away = [far[c, x, rows, :] for x in range(2)]
            if step > 0:
                for x in range(2):
                    line = 2 * c + x
                    away[x] = away[x] - v * far_lf[0, line : line + 1, :] - w * far_lf[1, line : line + 1, :]
            close = [near[c, x, rows, :] for x in range(2)]
            low = [jnp.where(odd, close[x], away[x]) for x in range(2)]
            high = [jnp.where(odd, away[x], close[x]) for x in range(2)]
            along = low + [u_ref[c, 0, rows, :], u_ref[c, 1, rows, :]] + high
            for x in range(2):
                b2, b1, a1, a2 = along[x], along[x + 1], along[x + 3], along[x + 4]
                adv = plus[x] * (0.25 * b2 - b1) + minus[x] * (a1 - 0.25 * a2)
                column = (2 * c + x) * LANES
                rhs[rows, column : column + LANES] = part_ref[c, x, rows, :] - new_weight[step] * adv
                if adv_ref is not None:
                    adv_ref[c, x, rows, :] = adv

    if step == 0:
        odd_y = lax.rem(own, 2) > 0
        for c, x in lines():
            low = jnp.where(odd_y, pair_y[c, x, 8:16, :], other_y[c, x, 8:16, :])
            high = jnp.where(odd_y, other_y[c, x, 0:8, :], pair_y[c, x, 0:8, :])
            y2, y1, w1, w2 = low[6:7], low[7:8], high[0:1], high[1:2]
            for row, viscous, up, down in (
                (0, y1, 0.25 * y2 - y1, None),
                (1, None, 0.25 * y1, None),
                (CY - 2, None, None, -0.25 * w1),
                (CY - 1, w1, None, w1 - 0.25 * w2),
            ):
                speed = u_ref[1, x, row : row + 1, :]
                if up is not None:
                    adv = 2.0 * courant[1] * jnp.maximum(speed, 0.0) * up
                else:
                    adv = 2.0 * courant[1] * jnp.minimum(speed, 0.0) * down
                adv_ref[c, x, row : row + 1, :] = adv_ref[c, x, row : row + 1, :] + adv
                change = -new_weight[step] * adv
                if viscous is not None:
                    change = change + (implicit_share[step] * stiff) * viscous
                column = slice((2 * c + x) * LANES, (2 * c + x + 1) * LANES)
                rhs[row : row + 1, column] = rhs[row : row + 1, column] + change

    inverse = inv_ref[...]
    first_flag = jnp.where(own > 0, 1.0, 0.0)
    last_flag = jnp.where(own < 7, 1.0, 0.0)
    coupling = -implicit_share[step] * stiff
    vw_ref[0] = jnp.broadcast_to(inverse[:, 0:1] * (coupling * first_flag), (CY, LANES))
    vw_ref[1] = jnp.broadcast_to(inverse[:, CY - 1 : CY] * (coupling * last_flag), (CY, LANES))

    def product(some, pair):
        return jnp.dot(
            some,
            rhs[:, pair * 256 : pair * 256 + 256],
            precision=lax.Precision.HIGHEST,
            preferred_element_type=jnp.float32,
        )

    outer = jnp.concatenate([inverse[0:8], inverse[CY - 8 : CY]], axis=0)
    found = [product(outer, pair) for pair in range(3)]

    def tile(row):
        at = row if row < 8 else row - CY + 16
        picked = [found[c][at : at + 1, x * LANES : (x + 1) * LANES] for c, x in lines()]
        return jnp.concatenate(picked + [vw_ref[0, row : row + 1, :], vw_ref[1, row : row + 1, :]], axis=0)

    if adv_ref is None:
        for t, row in enumerate((0, CY - 1)):
            for dest in range(8):
                send_ref[dest, t] = tile(row)
    else:
        for way, beside in enumerate((1, CY - 2)):
            for t, row in enumerate((0, CY - 1, beside)):
                packed[way, t] = tile(row)
        copies = [
            pltpu.make_async_copy(packed.at[jnp.where(own < dest, 1, 0)], send_ref.at[dest], sems.at[dest])
            for dest in range(8)
        ]
        for copy in copies:
            copy.start()
    for pair in range(3):
        solved = product(inverse, pair)
        g_ref[pair, 0] = solved[:, :LANES]
        g_ref[pair, 1] = solved[:, LANES:]
    if adv_ref is not None:
        for copy in copies:
            copy.wait()


def correct_kernel(step, got, g_ref, vw_ref, *refs):
    if step < SUBSTEPS - 1:
        u_ref, ends_ref, lf_ref, heads, tails = refs
    else:
        out_ref, heads, tails, u_ref, sems = refs
        ends_ref = None
    own = lax.axis_index("gy")
    shape = (8, LANES)
    zero = jnp.zeros(shape, jnp.float32)

    def tip(block, t, which):
        return jnp.broadcast_to(got[block, t, 6 + which : 7 + which, :], shape)

    for edge in (0, 1, 10, 11):
        heads[edge] = zero
        tails[edge] = zero
    prev_q, prev_last = zero, zero
    fronts, backs, front_qs, back_qs = [], [], [], []
    for block in range(8):
        head_v, tail_v, head_w, tail_w = tip(block, 0, 0), tip(block, 1, 0), tip(block, 0, 1), tip(block, 1, 1)
        pivot = 1.0 / (1.0 - head_v * prev_q)
        front = (got[block, 0] - head_v * prev_last) * pivot
        back = got[block, 1] - tail_v * prev_last + tail_v * prev_q * front
        front_q = head_w * pivot
        back_q = tail_w + tail_v * prev_q * front_q
        fronts.append(front)
        backs.append(back)
        front_qs.append(front_q)
        back_qs.append(back_q)
        prev_q, prev_last = back_q, back
    after = zero
    for block in range(7, -1, -1):
        head = fronts[block] - front_qs[block] * after
        heads[block + 2] = head
        tails[block + 2] = backs[block] - back_qs[block] * after
        after = head

    lower = tails[own + 1]
    upper = heads[own + 3]
    for c in range(3):
        for x in range(2):
            line = 2 * c + x
            low = lower[line : line + 1, :]
            high = upper[line : line + 1, :]
            u_ref[c, x] = g_ref[c, x] - vw_ref[0] * low - vw_ref[1] * high
        if ends_ref is None:
            pltpu.make_async_copy(u_ref.at[c], out_ref.at[c], sems.at[c]).start()
    if ends_ref is None:
        for c in range(3):
            pltpu.make_async_copy(u_ref.at[c], out_ref.at[c], sems.at[c]).wait()
    if ends_ref is not None:
        lf_ref[0] = lower
        lf_ref[1] = upper
        before = jnp.maximum(own - 1, 0)
        behind = jnp.minimum(own + 1, 7)
        row = got[before, 2]
        row = row - jnp.broadcast_to(got[before, 2, 6:7, :], shape) * tails[own]
        row = row - jnp.broadcast_to(got[before, 2, 7:8, :], shape) * heads[own + 2]
        ends_ref[0] = jnp.where(own > 0, row, zero)
        ends_ref[1] = lower
        ends_ref[2] = upper
        row = got[behind, 2]
        row = row - jnp.broadcast_to(got[behind, 2, 6:7, :], shape) * tails[own + 2]
        row = row - jnp.broadcast_to(got[behind, 2, 7:8, :], shape) * heads[own + 4]
        ends_ref[3] = jnp.where(own < 7, row, zero)


def f32(*shape):
    return pltpu.VMEM(shape, jnp.float32)


def call(kernel, arrays, outs, scratch, flops, scalars=(), large=(), hbm_outs=0):
    return pl.pallas_call(
        kernel,
        out_shape=outs,
        in_specs=[SMEM] * len(scalars) + [HBM] * len(large) + [VMEM] * len(arrays),
        out_specs=[VMEM] * (len(outs) - hbm_outs) + [HBM] * hbm_outs,
        scratch_shapes=scratch,
        cost_estimate=pl.CostEstimate(flops=flops, bytes_accessed=4 << 20, transcendentals=0),
        compiler_params=pltpu.CompilerParams(vmem_limit_bytes=16 << 20),
    )(
        *scalars,
        *[pltpu.with_memory_space_constraint(a, pltpu.HBM) for a in large],
        *[pltpu.with_memory_space_constraint(a, pltpu.VMEM) for a in arrays],
    )


def exchange(send):
    flat = send.reshape(8, send.shape[1] * 8, LANES)
    return lax.all_to_all(flat, "gy", split_axis=0, concat_axis=0).reshape(send.shape)


def scratch(*shape):
    return pltpu.VMEM(shape, jnp.float32)


def body(velocity, stiffness, block_inverse):
    gx = lax.axis_size("gx")
    gy = lax.axis_size("gy")
    field = f32(3, 2, CY, LANES)
    across = swaps(gx, 1, True)
    inside = swaps(gx, 0, True)
    for step in range(SUBSTEPS):
        last = step == SUBSTEPS - 1
        if step == 0:
            far = lax.ppermute(velocity, "gx", across)
            outs = [field, f32(3, 2, 16, LANES)]
            current, rows = call(pack_kernel, [], outs, [pltpu.SemaphoreType.DMA((3,))], 10**6, large=[velocity])
            pair_y = lax.ppermute(rows, "gy", swaps(gy, 0, False))
            other_y = lax.ppermute(rows, "gy", swaps(gy, 1, False))
            own_args = [current]
            more_args = [pair_y, other_y]
        else:
            far_lf = lax.ppermute(lf, "gx", across)
            own_args = [current, ends, share, adv]
            more_args = [far_lf, vw]
        near = lax.ppermute(current, "gx", inside)
        pad = [scratch(3, 2, CY + 16, LANES), pltpu.SemaphoreType.DMA]
        own = functools.partial(own_kernel, step)
        outs = [field, f32(CY, CY)] + [field] * (0 if last else 1)
        part, inverse, *shares = call(own, own_args, outs, pad, 10**8, [stiffness], [block_inverse])
        arrays = [current, far, near, part, inverse] + more_args
        planes = functools.partial(planes_kernel, step)
        edge = [scratch(CY, 6 * LANES)]
        if last:
            outs = [field, f32(2, CY, LANES), f32(8, 2, 8, LANES)]
        else:
            outs = [field, f32(2, CY, LANES), field, jax.ShapeDtypeStruct((8, 3, 8, LANES), jnp.float32)]
            edge += [scratch(2, 3, 8, LANES), pltpu.SemaphoreType.DMA((8,))]
        results = call(planes, arrays, outs, edge, 10**9, [stiffness], hbm_outs=0 if last else 1)
        g, vw, *advs, send = results
        got = exchange(send)
        if not last:
            share, adv = shares[0], advs[0]
            far = lax.ppermute(g, "gx", across)
        correct = functools.partial(correct_kernel, step)
        edge = [scratch(12, 8, LANES)] * 2
        if last:
            outs = [jax.ShapeDtypeStruct((3, 2, CY, LANES), jnp.float32)]
            edge = edge + [scratch(3, 2, CY, LANES), pltpu.SemaphoreType.DMA((3,))]
            return call(correct, [got, g, vw], outs, edge, 10**8, hbm_outs=1)[0]
        outs = [field, f32(4, 8, LANES), f32(2, 8, LANES)]
        current, ends, lf = call(correct, [got, g, vw], outs, edge, 10**8)


def solution(mesh):
    return jax.shard_map(
        body,
        mesh=mesh,
        in_specs=(P(None, "gx", "gy", None), P("gy"), P(None, "gy", None)),
        out_specs=P(None, "gx", "gy", None),
        check_vma=False,
    )
```

```python
import functools

import jax
import jax.numpy as jnp
from jax import lax
from jax.experimental import pallas as pl
from jax.experimental.pallas import tpu as pltpu
from jax.sharding import PartitionSpec as P


SUBSTEPS = 3
implicit_share = (8.0 / 15.0, 2.0 / 15.0, 1.0 / 3.0)
new_weight = (8.0 / 15.0, 5.0 / 12.0, 3.0 / 4.0)
old_weight = (0.0, -17.0 / 60.0, -5.0 / 12.0)
courant = (0.3, 0.2, 0.3)

CY = 192
LANES = 128
CHUNK = 32

VMEM = pl.BlockSpec(memory_space=pltpu.VMEM)
HBM = pl.BlockSpec(memory_space=pltpu.HBM)
SMEM = pl.BlockSpec(memory_space=pltpu.SMEM)


def swaps(count, offset, closed):
    pairs = []
    for a in range(offset, count + offset - 1, 2):
        b = a + 1
        if b < count:
            pairs += [(a, b), (b, a)]
        elif closed:
            pairs += [(a, 0), (0, a)]
    return pairs


def lines():
    return [(c, x) for c in range(3) for x in range(2)]


def pack_kernel(velocity, u_ref, rows_ref, sems):
    copies = [
        pltpu.make_async_copy(velocity.at[:, :, pl.ds(0, 8), :], rows_ref.at[:, :, pl.ds(0, 8), :], sems.at[0]),
        pltpu.make_async_copy(velocity.at[:, :, pl.ds(CY - 8, 8), :], rows_ref.at[:, :, pl.ds(8, 8), :], sems.at[1]),
        pltpu.make_async_copy(velocity, u_ref, sems.at[2]),
    ]
    for copy in copies:
        copy.start()
    for copy in copies:
        copy.wait()


def own_kernel(step, *refs):
    if step == 0:
        stiff_ref, inverses, u_ref, *refs = refs
        ends_ref = old_ref = None
    else:
        stiff_ref, inverses, u_ref, ends_ref, old_share, old_ref, _, *refs = refs
    if step < SUBSTEPS - 1:
        part_ref, inv_ref, share_ref, pad, sem = refs
    else:
        part_ref, inv_ref, pad, sem = refs
        share_ref = None
    fetch = pltpu.make_async_copy(inverses.at[step], inv_ref, sem)
    fetch.start()
    stiff = stiff_ref[0]

    for c in range(3):
        for x in range(2):
            pad[c, x, 8 : 8 + CY, :] = u_ref[c, x]
            if step == 0:
                pad[c, x, 0:8, :] = jnp.zeros((8, LANES), jnp.float32)
                pad[c, x, 8 + CY : 16 + CY, :] = jnp.zeros((8, LANES), jnp.float32)
            else:
                line = 2 * c + x
                pad[c, x, 6:7, :] = ends_ref[0, line : line + 1, :]
                pad[c, x, 7:8, :] = ends_ref[1, line : line + 1, :]
                pad[c, x, 8 + CY : 9 + CY, :] = ends_ref[2, line : line + 1, :]
                pad[c, x, 9 + CY : 10 + CY, :] = ends_ref[3, line : line + 1, :]

    for r in range(0, CY, CHUNK):
        rows = slice(r, r + CHUNK)
        for x in range(2):
            speed = [u_ref[d, x, rows, :] for d in range(3)]
            plus = [2.0 * courant[d] * jnp.maximum(speed[d], 0.0) for d in range(3)]
            minus = [2.0 * courant[d] * jnp.minimum(speed[d], 0.0) for d in range(3)]
            total = plus[0] - minus[0]
            for d in (1, 2):
                total = total + (plus[d] - minus[d])
            total = 0.75 * total
            for c in range(3):
                f = speed[c]
                adv = total * f
                y2, y1 = pad[c, x, 6 + r : 6 + r + CHUNK, :], pad[c, x, 7 + r : 7 + r + CHUNK, :]
                w1, w2 = pad[c, x, 9 + r : 9 + r + CHUNK, :], pad[c, x, 10 + r : 10 + r + CHUNK, :]
                adv = adv + plus[1] * (0.25 * y2 - y1) + minus[1] * (w1 - 0.25 * w2)
                z1, z2 = pltpu.roll(f, 1, 1), pltpu.roll(f, 2, 1)
                t1, t2 = pltpu.roll(f, LANES - 1, 1), pltpu.roll(f, LANES - 2, 1)
                adv = adv + plus[2] * (0.25 * z2 - z1) + minus[2] * (t1 - 0.25 * t2)
                forcing = f + (implicit_share[step] * stiff) * (w1 - 2.0 * f + y1) - new_weight[step] * adv
                if old_ref is not None:
                    old = old_share[c, x, rows, :] + old_ref[c, x, rows, :]
                    forcing = forcing - old_weight[step] * old
                part_ref[c, x, rows, :] = forcing
                if share_ref is not None:
                    share_ref[c, x, rows, :] = adv
    fetch.wait()


def planes_kernel(step, *refs):
    stiff_ref, u_ref, far, near, part_ref, inv_ref, *refs = refs
    if step > 0:
        far_lf, old_vw, *refs = refs
    else:
        pair_y, other_y, *refs = refs
    if step < SUBSTEPS - 1:
        g_ref, vw_ref, adv_ref, send_ref, rhs, packed, sems = refs
    else:
        g_ref, vw_ref, send_ref, rhs = refs
        adv_ref = None
    own = lax.axis_index("gy")
    odd = lax.rem(lax.axis_index("gx"), 2) > 0
    partner = jnp.where(odd, 1, 0)
    stiff = stiff_ref[0]

    for r in range(0, CY, CHUNK):
        rows = slice(r, r + CHUNK)
        plus = [2.0 * courant[0] * jnp.maximum(u_ref[0, x, rows, :], 0.0) for x in range(2)]
        minus = [2.0 * courant[0] * jnp.minimum(u_ref[0, x, rows, :], 0.0) for x in range(2)]
        if step > 0:
            v, w = old_vw[0, rows, :], old_vw[1, rows, :]
            low_far, high_far = far_lf[partner, 0], far_lf[partner, 1]
        for c in range(3):
            away = [far[c, x, rows, :] for x in range(2)]
            if step > 0:
                for x in range(2):
                    line = 2 * c + x
                    away[x] = away[x] - v * low_far[line : line + 1, :] - w * high_far[line : line + 1, :]
            close = [near[c, x, rows, :] for x in range(2)]
            low = [jnp.where(odd, close[x], away[x]) for x in range(2)]
            high = [jnp.where(odd, away[x], close[x]) for x in range(2)]
            along = low + [u_ref[c, 0, rows, :], u_ref[c, 1, rows, :]] + high
            for x in range(2):
                b2, b1, a1, a2 = along[x], along[x + 1], along[x + 3], along[x + 4]
                adv = plus[x] * (0.25 * b2 - b1) + minus[x] * (a1 - 0.25 * a2)
                column = (2 * c + x) * LANES
                rhs[rows, column : column + LANES] = part_ref[c, x, rows, :] - new_weight[step] * adv
                if adv_ref is not None:
                    adv_ref[c, x, rows, :] = adv

    if step == 0:
        odd_y = lax.rem(own, 2) > 0
        for c, x in lines():
            low = jnp.where(odd_y, pair_y[c, x, 8:16, :], other_y[c, x, 8:16, :])
            high = jnp.where(odd_y, other_y[c, x, 0:8, :], pair_y[c, x, 0:8, :])
            y2, y1, w1, w2 = low[6:7], low[7:8], high[0:1], high[1:2]
            for row, viscous, up, down in (
                (0, y1, 0.25 * y2 - y1, None),
                (1, None, 0.25 * y1, None),
                (CY - 2, None, None, -0.25 * w1),
                (CY - 1, w1, None, w1 - 0.25 * w2),
            ):
                speed = u_ref[1, x, row : row + 1, :]
                if up is not None:
                    adv = 2.0 * courant[1] * jnp.maximum(speed, 0.0) * up
                else:
                    adv = 2.0 * courant[1] * jnp.minimum(speed, 0.0) * down
                adv_ref[c, x, row : row + 1, :] = adv_ref[c, x, row : row + 1, :] + adv
                change = -new_weight[step] * adv
                if viscous is not None:
                    change = change + (implicit_share[step] * stiff) * viscous
                column = slice((2 * c + x) * LANES, (2 * c + x + 1) * LANES)
                rhs[row : row + 1, column] = rhs[row : row + 1, column] + change

    inverse = inv_ref[...]
    first_flag = jnp.where(own > 0, 1.0, 0.0)
    last_flag = jnp.where(own < 7, 1.0, 0.0)
    coupling = -implicit_share[step] * stiff
    vw_ref[0] = jnp.broadcast_to(inverse[:, 0:1] * (coupling * first_flag), (CY, LANES))
    vw_ref[1] = jnp.broadcast_to(inverse[:, CY - 1 : CY] * (coupling * last_flag), (CY, LANES))

    def product(some, pair):
        return jnp.dot(
            some,
            rhs[:, pair * 256 : pair * 256 + 256],
            precision=lax.Precision.HIGHEST,
            preferred_element_type=jnp.float32,
        )

    def tile(row, pick):
        picked = [pick(c, x, row) for c, x in lines()]
        return jnp.concatenate(picked + [vw_ref[0, row : row + 1, :], vw_ref[1, row : row + 1, :]], axis=0)

    if adv_ref is not None:
        outer = jnp.concatenate([inverse[0:8], inverse[CY - 8 : CY]], axis=0)
        found = [product(outer, pair) for pair in range(3)]

        def outermost(c, x, row):
            at = row if row < 8 else row - CY + 16
            return found[c][at : at + 1, x * LANES : (x + 1) * LANES]

        for way, beside in enumerate((1, CY - 2)):
            for t, row in enumerate((0, CY - 1, beside)):
                packed[way, t] = tile(row, outermost)
        copies = [
            pltpu.make_async_copy(packed.at[jnp.where(own < dest, 1, 0)], send_ref.at[dest], sems.at[dest])
            for dest in range(8)
        ]
        for copy in copies:
            copy.start()

        @pl.when(own >= 0)
        def _():
            for pair in range(3):
                solved = product(inv_ref[...], pair)
                g_ref[pair, 0] = solved[:, :LANES]
                g_ref[pair, 1] = solved[:, LANES:]

        for copy in copies:
            copy.wait()
    else:
        for pair in range(3):
            solved = product(inverse, pair)
            g_ref[pair, 0] = solved[:, :LANES]
            g_ref[pair, 1] = solved[:, LANES:]
        for t, row in enumerate((0, CY - 1)):
            ends = tile(row, lambda c, x, row: g_ref[c, x, row : row + 1, :])
            for dest in range(8):
                send_ref[dest, t] = ends


def correct_kernel(step, got, g_ref, vw_ref, *refs):
    if step < SUBSTEPS - 1:
        u_ref, ends_ref, lf_ref, heads, tails = refs
    else:
        out_ref, heads, tails, u_ref, sems = refs
        ends_ref = None
    own = lax.axis_index("gy")
    shape = (8, LANES)
    zero = jnp.zeros(shape, jnp.float32)

    def tip(block, t, which):
        return jnp.broadcast_to(got[block, t, 6 + which : 7 + which, :], shape)

    for edge in (0, 1, 10, 11):
        heads[edge] = zero
        tails[edge] = zero
    prev_q, prev_last = zero, zero
    fronts, backs, front_qs, back_qs = [], [], [], []
    for block in range(8):
        head_v, tail_v, head_w, tail_w = tip(block, 0, 0), tip(block, 1, 0), tip(block, 0, 1), tip(block, 1, 1)
        pivot = 1.0 / (1.0 - head_v * prev_q)
        front = (got[block, 0] - head_v * prev_last) * pivot
        back = got[block, 1] - tail_v * prev_last + tail_v * prev_q * front
        front_q = head_w * pivot
        back_q = tail_w + tail_v * prev_q * front_q
        fronts.append(front)
        backs.append(back)
        front_qs.append(front_q)
        back_qs.append(back_q)
        prev_q, prev_last = back_q, back
    after = zero
    for block in range(7, -1, -1):
        head = fronts[block] - front_qs[block] * after
        heads[block + 2] = head
        tails[block + 2] = backs[block] - back_qs[block] * after
        after = head

    lower = tails[own + 1]
    upper = heads[own + 3]
    for c in range(3):
        for x in range(2):
            line = 2 * c + x
            low = lower[line : line + 1, :]
            high = upper[line : line + 1, :]
            u_ref[c, x] = g_ref[c, x] - vw_ref[0] * low - vw_ref[1] * high
        if ends_ref is None:
            pltpu.make_async_copy(u_ref.at[c], out_ref.at[c], sems.at[c]).start()
    if ends_ref is None:
        for c in range(3):
            pltpu.make_async_copy(u_ref.at[c], out_ref.at[c], sems.at[c]).wait()
    if ends_ref is not None:
        for side in range(2):
            lf_ref[side, 0] = lower
            lf_ref[side, 1] = upper
        before = jnp.maximum(own - 1, 0)
        behind = jnp.minimum(own + 1, 7)
        row = got[before, 2]
        row = row - jnp.broadcast_to(got[before, 2, 6:7, :], shape) * tails[own]
        row = row - jnp.broadcast_to(got[before, 2, 7:8, :], shape) * heads[own + 2]
        ends_ref[0] = jnp.where(own > 0, row, zero)
        ends_ref[1] = lower
        ends_ref[2] = upper
        row = got[behind, 2]
        row = row - jnp.broadcast_to(got[behind, 2, 6:7, :], shape) * tails[own + 2]
        row = row - jnp.broadcast_to(got[behind, 2, 7:8, :], shape) * heads[own + 4]
        ends_ref[3] = jnp.where(own < 7, row, zero)


def f32(*shape):
    return pltpu.VMEM(shape, jnp.float32)


def call(kernel, arrays, outs, scratch, flops, scalars=(), large=(), hbm_outs=0):
    return pl.pallas_call(
        kernel,
        out_shape=outs,
        in_specs=[SMEM] * len(scalars) + [HBM] * len(large) + [VMEM] * len(arrays),
        out_specs=[VMEM] * (len(outs) - hbm_outs) + [HBM] * hbm_outs,
        scratch_shapes=scratch,
        cost_estimate=pl.CostEstimate(flops=flops, bytes_accessed=4 << 20, transcendentals=0),
        compiler_params=pltpu.CompilerParams(vmem_limit_bytes=16 << 20),
    )(
        *scalars,
        *[pltpu.with_memory_space_constraint(a, pltpu.HBM) for a in large],
        *[pltpu.with_memory_space_constraint(a, pltpu.VMEM) for a in arrays],
    )


def exchange(send):
    flat = send.reshape(8, send.shape[1] * 8, LANES)
    return lax.all_to_all(flat, "gy", split_axis=0, concat_axis=0).reshape(send.shape)


def scratch(*shape):
    return pltpu.VMEM(shape, jnp.float32)


def body(velocity, stiffness, block_inverse):
    gx = lax.axis_size("gx")
    gy = lax.axis_size("gy")
    field = f32(3, 2, CY, LANES)
    across = swaps(gx, 1, True)
    inside = swaps(gx, 0, True)
    for step in range(SUBSTEPS):
        last = step == SUBSTEPS - 1
        if step == 0:
            far = lax.ppermute(velocity, "gx", across)
            outs = [field, f32(3, 2, 16, LANES)]
            current, rows = call(pack_kernel, [], outs, [pltpu.SemaphoreType.DMA((3,))], 10**6, large=[velocity])
            pair_y = lax.ppermute(rows, "gy", swaps(gy, 0, False))
            other_y = lax.ppermute(rows, "gy", swaps(gy, 1, False))
            own_args = [current]
            more_args = [pair_y, other_y]
        else:
            pairs = [[a, (a + 1) % gx] for a in range(1, gx, 2)]
            far_lf = lax.all_to_all(
                lf.reshape(2, 16, LANES), "gx", split_axis=0, concat_axis=0, axis_index_groups=pairs
            ).reshape(2, 2, 8, LANES)
            own_args = [current, ends, share, adv, far_lf]
            more_args = [far_lf, vw]
        near = lax.ppermute(current, "gx", inside)
        pad = [scratch(3, 2, CY + 16, LANES), pltpu.SemaphoreType.DMA]
        own = functools.partial(own_kernel, step)
        outs = [field, f32(CY, CY)] + [field] * (0 if last else 1)
        part, inverse, *shares = call(own, own_args, outs, pad, 10**8, [stiffness], [block_inverse])
        arrays = [current, far, near, part, inverse] + more_args
        planes = functools.partial(planes_kernel, step)
        edge = [scratch(CY, 6 * LANES)]
        if last:
            outs = [field, f32(2, CY, LANES), f32(8, 2, 8, LANES)]
        else:
            outs = [field, f32(2, CY, LANES), field, jax.ShapeDtypeStruct((8, 3, 8, LANES), jnp.float32)]
            edge += [scratch(2, 3, 8, LANES), pltpu.SemaphoreType.DMA((8,))]
        results = call(planes, arrays, outs, edge, 10**9, [stiffness], hbm_outs=0 if last else 1)
        g, vw, *advs, send = results
        got = exchange(send)
        if not last:
            share, adv = shares[0], advs[0]
            far = lax.ppermute(g, "gx", across)
        correct = functools.partial(correct_kernel, step)
        edge = [scratch(12, 8, LANES)] * 2
        if last:
            outs = [jax.ShapeDtypeStruct((3, 2, CY, LANES), jnp.float32)]
            edge = edge + [scratch(3, 2, CY, LANES), pltpu.SemaphoreType.DMA((3,))]
            return call(correct, [got, g, vw], outs, edge, 10**8, hbm_outs=1)[0]
        outs = [field, f32(4, 8, LANES), f32(2, 2, 8, LANES)]
        current, ends, lf = call(correct, [got, g, vw], outs, edge, 10**8)


def solution(mesh):
    return jax.shard_map(
        body,
        mesh=mesh,
        in_specs=(P(None, "gx", "gy", None), P("gy"), P(None, "gy", None)),
        out_specs=P(None, "gx", "gy", None),
        check_vma=False,
    )
```

```python
import functools

import jax
import jax.numpy as jnp
from jax import lax
from jax.experimental import pallas as pl
from jax.experimental.pallas import tpu as pltpu
from jax.sharding import PartitionSpec as P


SUBSTEPS = 3
implicit_share = (8.0 / 15.0, 2.0 / 15.0, 1.0 / 3.0)
new_weight = (8.0 / 15.0, 5.0 / 12.0, 3.0 / 4.0)
old_weight = (0.0, -17.0 / 60.0, -5.0 / 12.0)
courant = (0.3, 0.2, 0.3)

CY = 192
LANES = 128
CHUNK = 32

VMEM = pl.BlockSpec(memory_space=pltpu.VMEM)
HBM = pl.BlockSpec(memory_space=pltpu.HBM)
SMEM = pl.BlockSpec(memory_space=pltpu.SMEM)


def swaps(count, offset, closed):
    pairs = []
    for a in range(offset, count + offset - 1, 2):
        b = a + 1
        if b < count:
            pairs += [(a, b), (b, a)]
        elif closed:
            pairs += [(a, 0), (0, a)]
    return pairs


def lines():
    return [(c, x) for c in range(3) for x in range(2)]


def pack_kernel(velocity, u_ref, rows_ref, sems):
    copies = [
        pltpu.make_async_copy(velocity.at[:, :, pl.ds(0, 8), :], rows_ref.at[:, :, pl.ds(0, 8), :], sems.at[0]),
        pltpu.make_async_copy(velocity.at[:, :, pl.ds(CY - 8, 8), :], rows_ref.at[:, :, pl.ds(8, 8), :], sems.at[1]),
        pltpu.make_async_copy(velocity, u_ref, sems.at[2]),
    ]
    for copy in copies:
        copy.start()
    for copy in copies:
        copy.wait()


def own_kernel(step, *refs):
    if step == 0:
        stiff_ref, inverses, u_ref, *refs = refs
        ends_ref = old_ref = None
    else:
        stiff_ref, inverses, u_ref, ends_ref, old_share, old_ref, *refs = refs
    if step < SUBSTEPS - 1:
        part_ref, inv_ref, share_ref, pad, sem = refs
    else:
        part_ref, inv_ref, pad, sem = refs
        share_ref = None
    fetch = pltpu.make_async_copy(inverses.at[step], inv_ref, sem)
    fetch.start()
    stiff = stiff_ref[0]

    for c in range(3):
        for x in range(2):
            pad[c, x, 8 : 8 + CY, :] = u_ref[c, x]
            if step == 0:
                pad[c, x, 0:8, :] = jnp.zeros((8, LANES), jnp.float32)
                pad[c, x, 8 + CY : 16 + CY, :] = jnp.zeros((8, LANES), jnp.float32)
            else:
                line = 2 * c + x
                pad[c, x, 6:7, :] = ends_ref[0, line : line + 1, :]
                pad[c, x, 7:8, :] = ends_ref[1, line : line + 1, :]
                pad[c, x, 8 + CY : 9 + CY, :] = ends_ref[2, line : line + 1, :]
                pad[c, x, 9 + CY : 10 + CY, :] = ends_ref[3, line : line + 1, :]

    for r in range(0, CY, CHUNK):
        rows = slice(r, r + CHUNK)
        for x in range(2):
            speed = [u_ref[d, x, rows, :] for d in range(3)]
            plus = [2.0 * courant[d] * jnp.maximum(speed[d], 0.0) for d in range(3)]
            minus = [2.0 * courant[d] * jnp.minimum(speed[d], 0.0) for d in range(3)]
            total = plus[0] - minus[0]
            for d in (1, 2):
                total = total + (plus[d] - minus[d])
            total = 0.75 * total
            for c in range(3):
                f = speed[c]
                adv = total * f
                y2, y1 = pad[c, x, 6 + r : 6 + r + CHUNK, :], pad[c, x, 7 + r : 7 + r + CHUNK, :]
                w1, w2 = pad[c, x, 9 + r : 9 + r + CHUNK, :], pad[c, x, 10 + r : 10 + r + CHUNK, :]
                adv = adv + plus[1] * (0.25 * y2 - y1) + minus[1] * (w1 - 0.25 * w2)
                z1, z2 = pltpu.roll(f, 1, 1), pltpu.roll(f, 2, 1)
                t1, t2 = pltpu.roll(f, LANES - 1, 1), pltpu.roll(f, LANES - 2, 1)
                adv = adv + plus[2] * (0.25 * z2 - z1) + minus[2] * (t1 - 0.25 * t2)
                forcing = f + (implicit_share[step] * stiff) * (w1 - 2.0 * f + y1) - new_weight[step] * adv
                if old_ref is not None:
                    old = old_share[c, x, rows, :] + old_ref[c, x, rows, :]
                    forcing = forcing - old_weight[step] * old
                part_ref[c, x, rows, :] = forcing
                if share_ref is not None:
                    share_ref[c, x, rows, :] = adv
    fetch.wait()


def planes_kernel(step, *refs):
    stiff_ref, u_ref, far, near, part_ref, inv_ref, *refs = refs
    if step > 0:
        far_lf, old_vw, *refs = refs
    else:
        pair_y, other_y, *refs = refs
    if step < SUBSTEPS - 1:
        g_ref, vw_ref, adv_ref, send_ref, rhs, packed, sems = refs
    else:
        g_ref, vw_ref, send_ref, rhs = refs
        adv_ref = None
    own = lax.axis_index("gy")
    odd = lax.rem(lax.axis_index("gx"), 2) > 0
    stiff = stiff_ref[0]

    for r in range(0, CY, CHUNK):
        rows = slice(r, r + CHUNK)
        plus = [2.0 * courant[0] * jnp.maximum(u_ref[0, x, rows, :], 0.0) for x in range(2)]
        minus = [2.0 * courant[0] * jnp.minimum(u_ref[0, x, rows, :], 0.0) for x in range(2)]
        if step > 0:
            v, w = old_vw[0, rows, :], old_vw[1, rows, :]
        for c in range(3):
            away = [far[c, x, rows, :] for x in range(2)]
            if step > 0:
                for x in range(2):
                    line = 2 * c + x
                    away[x] = away[x] - v * far_lf[0, line : line + 1, :] - w * far_lf[1, line : line + 1, :]
            close = [near[c, x, rows, :] for x in range(2)]
            low = [jnp.where(odd, close[x], away[x]) for x in range(2)]
            high = [jnp.where(odd, away[x], close[x]) for x in range(2)]
            along = low + [u_ref[c, 0, rows, :], u_ref[c, 1, rows, :]] + high
            for x in range(2):
                b2, b1, a1, a2 = along[x], along[x + 1], along[x + 3], along[x + 4]
                adv = plus[x] * (0.25 * b2 - b1) + minus[x] * (a1 - 0.25 * a2)
                column = (2 * c + x) * LANES
                rhs[rows, column : column + LANES] = part_ref[c, x, rows, :] - new_weight[step] * adv
                if adv_ref is not None:
                    adv_ref[c, x, rows, :] = adv

    if step == 0:
        odd_y = lax.rem(own, 2) > 0
        for c, x in lines():
            low = jnp.where(odd_y, pair_y[c, x, 8:16, :], other_y[c, x, 8:16, :])
            high = jnp.where(odd_y, other_y[c, x, 0:8, :], pair_y[c, x, 0:8, :])
            y2, y1, w1, w2 = low[6:7], low[7:8], high[0:1], high[1:2]
            for row, viscous, up, down in (
                (0, y1, 0.25 * y2 - y1, None),
                (1, None, 0.25 * y1, None),
                (CY - 2, None, None, -0.25 * w1),
                (CY - 1, w1, None, w1 - 0.25 * w2),
            ):
                speed = u_ref[1, x, row : row + 1, :]
                if up is not None:
                    adv = 2.0 * courant[1] * jnp.maximum(speed, 0.0) * up
                else:
                    adv = 2.0 * courant[1] * jnp.minimum(speed, 0.0) * down
                adv_ref[c, x, row : row + 1, :] = adv_ref[c, x, row : row + 1, :] + adv
                change = -new_weight[step] * adv
                if viscous is not None:
                    change = change + (implicit_share[step] * stiff) * viscous
                column = slice((2 * c + x) * LANES, (2 * c + x + 1) * LANES)
                rhs[row : row + 1, column] = rhs[row : row + 1, column] + change

    inverse = inv_ref[...]
    first_flag = jnp.where(own > 0, 1.0, 0.0)
    last_flag = jnp.where(own < 7, 1.0, 0.0)
    coupling = -implicit_share[step] * stiff
    vw_ref[0] = jnp.broadcast_to(inverse[:, 0:1] * (coupling * first_flag), (CY, LANES))
    vw_ref[1] = jnp.broadcast_to(inverse[:, CY - 1 : CY] * (coupling * last_flag), (CY, LANES))

    def product(some, pair):
        return jnp.dot(
            some,
            rhs[:, pair * 256 : pair * 256 + 256],
            precision=lax.Precision.HIGHEST,
            preferred_element_type=jnp.float32,
        )

    def tile(row, pick):
        picked = [pick(c, x, row) for c, x in lines()]
        return jnp.concatenate(picked + [vw_ref[0, row : row + 1, :], vw_ref[1, row : row + 1, :]], axis=0)

    if adv_ref is not None:
        outer = jnp.concatenate([inverse[0:8], inverse[CY - 8 : CY]], axis=0)
        found = [product(outer, pair) for pair in range(3)]

        def outermost(c, x, row):
            at = row if row < 8 else row - CY + 16
            return found[c][at : at + 1, x * LANES : (x + 1) * LANES]

        for way, beside in enumerate((1, CY - 2)):
            for t, row in enumerate((0, CY - 1, beside)):
                packed[way, t] = tile(row, outermost)
        copies = [
            pltpu.make_async_copy(packed.at[jnp.where(own < dest, 1, 0)], send_ref.at[dest], sems.at[dest])
            for dest in range(8)
        ]
        for copy in copies:
            copy.start()

        @pl.when(own >= 0)
        def _():
            for pair in range(3):
                solved = product(inv_ref[...], pair)
                g_ref[pair, 0] = solved[:, :LANES]
                g_ref[pair, 1] = solved[:, LANES:]

        for copy in copies:
            copy.wait()
    else:
        for pair in range(3):
            solved = product(inverse, pair)
            g_ref[pair, 0] = solved[:, :LANES]
            g_ref[pair, 1] = solved[:, LANES:]
        for t, row in enumerate((0, CY - 1)):
            ends = tile(row, lambda c, x, row: g_ref[c, x, row : row + 1, :])
            for dest in range(8):
                send_ref[dest, t] = ends


def correct_kernel(step, got, g_ref, vw_ref, *refs):
    if step < SUBSTEPS - 1:
        u_ref, ends_ref, lf_ref, heads, tails = refs
    else:
        out_ref, heads, tails, u_ref, sems = refs
        ends_ref = None
    own = lax.axis_index("gy")
    shape = (8, LANES)
    zero = jnp.zeros(shape, jnp.float32)

    def tip(block, t, which):
        return jnp.broadcast_to(got[block, t, 6 + which : 7 + which, :], shape)

    for edge in (0, 1, 10, 11):
        heads[edge] = zero
        tails[edge] = zero
    prev_q, prev_last = zero, zero
    fronts, backs, front_qs, back_qs = [], [], [], []
    for block in range(8):
        head_v, tail_v, head_w, tail_w = tip(block, 0, 0), tip(block, 1, 0), tip(block, 0, 1), tip(block, 1, 1)
        pivot = 1.0 / (1.0 - head_v * prev_q)
        front = (got[block, 0] - head_v * prev_last) * pivot
        back = got[block, 1] - tail_v * prev_last + tail_v * prev_q * front
        front_q = head_w * pivot
        back_q = tail_w + tail_v * prev_q * front_q
        fronts.append(front)
        backs.append(back)
        front_qs.append(front_q)
        back_qs.append(back_q)
        prev_q, prev_last = back_q, back
    after = zero
    for block in range(7, -1, -1):
        head = fronts[block] - front_qs[block] * after
        heads[block + 2] = head
        tails[block + 2] = backs[block] - back_qs[block] * after
        after = head

    lower = tails[own + 1]
    upper = heads[own + 3]
    for c in range(3):
        for x in range(2):
            line = 2 * c + x
            low = lower[line : line + 1, :]
            high = upper[line : line + 1, :]
            u_ref[c, x] = g_ref[c, x] - vw_ref[0] * low - vw_ref[1] * high
        if ends_ref is None:
            pltpu.make_async_copy(u_ref.at[c], out_ref.at[c], sems.at[c]).start()
    if ends_ref is None:
        for c in range(3):
            pltpu.make_async_copy(u_ref.at[c], out_ref.at[c], sems.at[c]).wait()
    if ends_ref is not None:
        lf_ref[0] = lower
        lf_ref[1] = upper
        before = jnp.maximum(own - 1, 0)
        behind = jnp.minimum(own + 1, 7)
        row = got[before, 2]
        row = row - jnp.broadcast_to(got[before, 2, 6:7, :], shape) * tails[own]
        row = row - jnp.broadcast_to(got[before, 2, 7:8, :], shape) * heads[own + 2]
        ends_ref[0] = jnp.where(own > 0, row, zero)
        ends_ref[1] = lower
        ends_ref[2] = upper
        row = got[behind, 2]
        row = row - jnp.broadcast_to(got[behind, 2, 6:7, :], shape) * tails[own + 2]
        row = row - jnp.broadcast_to(got[behind, 2, 7:8, :], shape) * heads[own + 4]
        ends_ref[3] = jnp.where(own < 7, row, zero)


def f32(*shape):
    return pltpu.VMEM(shape, jnp.float32)


def call(kernel, arrays, outs, scratch, flops, scalars=(), large=(), hbm_outs=0):
    return pl.pallas_call(
        kernel,
        out_shape=outs,
        in_specs=[SMEM] * len(scalars) + [HBM] * len(large) + [VMEM] * len(arrays),
        out_specs=[VMEM] * (len(outs) - hbm_outs) + [HBM] * hbm_outs,
        scratch_shapes=scratch,
        cost_estimate=pl.CostEstimate(flops=flops, bytes_accessed=4 << 20, transcendentals=0),
        compiler_params=pltpu.CompilerParams(vmem_limit_bytes=16 << 20),
    )(
        *scalars,
        *[pltpu.with_memory_space_constraint(a, pltpu.HBM) for a in large],
        *[pltpu.with_memory_space_constraint(a, pltpu.VMEM) for a in arrays],
    )


def exchange(send):
    flat = send.reshape(8, send.shape[1] * 8, LANES)
    return lax.all_to_all(flat, "gy", split_axis=0, concat_axis=0).reshape(send.shape)


def scratch(*shape):
    return pltpu.VMEM(shape, jnp.float32)


def body(velocity, stiffness, block_inverse):
    gx = lax.axis_size("gx")
    gy = lax.axis_size("gy")
    field = f32(3, 2, CY, LANES)
    across = swaps(gx, 1, True)
    inside = swaps(gx, 0, True)
    for step in range(SUBSTEPS):
        last = step == SUBSTEPS - 1
        if step == 0:
            far = lax.ppermute(velocity, "gx", across)
            outs = [field, f32(3, 2, 16, LANES)]
            current, rows = call(pack_kernel, [], outs, [pltpu.SemaphoreType.DMA((3,))], 10**6, large=[velocity])
            pair_y = lax.ppermute(rows, "gy", swaps(gy, 0, False))
            other_y = lax.ppermute(rows, "gy", swaps(gy, 1, False))
            own_args = [current]
            more_args = [pair_y, other_y]
        else:
            far_lf = lax.ppermute(lf, "gx", across)
            own_args = [current, ends, share, adv]
            more_args = [far_lf, vw]
        near = lax.ppermute(current, "gx", inside)
        pad = [scratch(3, 2, CY + 16, LANES), pltpu.SemaphoreType.DMA]
        own = functools.partial(own_kernel, step)
        outs = [field, f32(CY, CY)] + [field] * (0 if last else 1)
        part, inverse, *shares = call(own, own_args, outs, pad, 10**8, [stiffness], [block_inverse])
        arrays = [current, far, near, part, inverse] + more_args
        planes = functools.partial(planes_kernel, step)
        edge = [scratch(CY, 6 * LANES)]
        if last:
            outs = [field, f32(2, CY, LANES), f32(8, 2, 8, LANES)]
        else:
            outs = [field, f32(2, CY, LANES), field, jax.ShapeDtypeStruct((8, 3, 8, LANES), jnp.float32)]
            edge += [scratch(2, 3, 8, LANES), pltpu.SemaphoreType.DMA((8,))]
        results = call(planes, arrays, outs, edge, 10**9, [stiffness], hbm_outs=0 if last else 1)
        g, vw, *advs, send = results
        got = exchange(send)
        if not last:
            share, adv = shares[0], advs[0]
            far = lax.ppermute(g, "gx", across)
        correct = functools.partial(correct_kernel, step)
        edge = [scratch(12, 8, LANES)] * 2
        if last:
            outs = [jax.ShapeDtypeStruct((3, 2, CY, LANES), jnp.float32)]
            edge = edge + [scratch(3, 2, CY, LANES), pltpu.SemaphoreType.DMA((3,))]
            return call(correct, [got, g, vw], outs, edge, 10**8, hbm_outs=1)[0]
        outs = [field, f32(4, 8, LANES), f32(2, 8, LANES)]
        current, ends, lf = call(correct, [got, g, vw], outs, edge, 10**8)


def solution(mesh):
    return jax.shard_map(
        body,
        mesh=mesh,
        in_specs=(P(None, "gx", "gy", None), P("gy"), P(None, "gy", None)),
        out_specs=P(None, "gx", "gy", None),
        check_vma=False,
    )
```

```python
import functools

import jax
import jax.numpy as jnp
from jax import lax
from jax.experimental import pallas as pl
from jax.experimental.pallas import tpu as pltpu
from jax.sharding import PartitionSpec as P


SUBSTEPS = 3
implicit_share = (8.0 / 15.0, 2.0 / 15.0, 1.0 / 3.0)
new_weight = (8.0 / 15.0, 5.0 / 12.0, 3.0 / 4.0)
old_weight = (0.0, -17.0 / 60.0, -5.0 / 12.0)
courant = (0.3, 0.2, 0.3)

CY = 192
LANES = 128
CHUNK = 32

VMEM = pl.BlockSpec(memory_space=pltpu.VMEM)
HBM = pl.BlockSpec(memory_space=pltpu.HBM)
SMEM = pl.BlockSpec(memory_space=pltpu.SMEM)


def swaps(count, offset, closed):
    pairs = []
    for a in range(offset, count + offset - 1, 2):
        b = a + 1
        if b < count:
            pairs += [(a, b), (b, a)]
        elif closed:
            pairs += [(a, 0), (0, a)]
    return pairs


def lines():
    return [(c, x) for c in range(3) for x in range(2)]


def pack_kernel(velocity, u_ref, top_ref, bottom_ref, sems):
    copies = [
        pltpu.make_async_copy(velocity.at[:, :, pl.ds(0, 8), :], top_ref, sems.at[0]),
        pltpu.make_async_copy(velocity.at[:, :, pl.ds(CY - 8, 8), :], bottom_ref, sems.at[1]),
        pltpu.make_async_copy(velocity, u_ref, sems.at[2]),
    ]
    for copy in copies:
        copy.start()
    for copy in copies:
        copy.wait()


def own_kernel(step, *refs):
    if step == 0:
        stiff_ref, inverses, u_ref, *refs = refs
        ends_ref = old_ref = None
    else:
        stiff_ref, inverses, u_ref, ends_ref, old_share, old_ref, *refs = refs
    if step < SUBSTEPS - 1:
        part_ref, inv_ref, share_ref, pad, sem = refs
    else:
        part_ref, inv_ref, pad, sem = refs
        share_ref = None
    fetch = pltpu.make_async_copy(inverses.at[step], inv_ref, sem)
    fetch.start()
    stiff = stiff_ref[0]

    for c in range(3):
        for x in range(2):
            pad[c, x, 8 : 8 + CY, :] = u_ref[c, x]
            if step == 0:
                pad[c, x, 0:8, :] = jnp.zeros((8, LANES), jnp.float32)
                pad[c, x, 8 + CY : 16 + CY, :] = jnp.zeros((8, LANES), jnp.float32)
            else:
                line = 2 * c + x
                pad[c, x, 6:7, :] = ends_ref[0, line : line + 1, :]
                pad[c, x, 7:8, :] = ends_ref[1, line : line + 1, :]
                pad[c, x, 8 + CY : 9 + CY, :] = ends_ref[2, line : line + 1, :]
                pad[c, x, 9 + CY : 10 + CY, :] = ends_ref[3, line : line + 1, :]

    for r in range(0, CY, CHUNK):
        rows = slice(r, r + CHUNK)
        for x in range(2):
            speed = [u_ref[d, x, rows, :] for d in range(3)]
            plus = [2.0 * courant[d] * jnp.maximum(speed[d], 0.0) for d in range(3)]
            minus = [2.0 * courant[d] * jnp.minimum(speed[d], 0.0) for d in range(3)]
            total = plus[0] - minus[0]
            for d in (1, 2):
                total = total + (plus[d] - minus[d])
            total = 0.75 * total
            for c in range(3):
                f = speed[c]
                adv = total * f
                y2, y1 = pad[c, x, 6 + r : 6 + r + CHUNK, :], pad[c, x, 7 + r : 7 + r + CHUNK, :]
                w1, w2 = pad[c, x, 9 + r : 9 + r + CHUNK, :], pad[c, x, 10 + r : 10 + r + CHUNK, :]
                adv = adv + plus[1] * (0.25 * y2 - y1) + minus[1] * (w1 - 0.25 * w2)
                z1, z2 = pltpu.roll(f, 1, 1), pltpu.roll(f, 2, 1)
                t1, t2 = pltpu.roll(f, LANES - 1, 1), pltpu.roll(f, LANES - 2, 1)
                adv = adv + plus[2] * (0.25 * z2 - z1) + minus[2] * (t1 - 0.25 * t2)
                forcing = f + (implicit_share[step] * stiff) * (w1 - 2.0 * f + y1) - new_weight[step] * adv
                if old_ref is not None:
                    old = old_share[c, x, rows, :] + old_ref[c, x, rows, :]
                    forcing = forcing - old_weight[step] * old
                part_ref[c, x, rows, :] = forcing
                if share_ref is not None:
                    share_ref[c, x, rows, :] = adv
    fetch.wait()


def planes_kernel(step, *refs):
    stiff_ref, u_ref, far, near, part_ref, inv_ref, *refs = refs
    if step > 0:
        far_lf, old_vw, *refs = refs
    else:
        before, behind, *refs = refs
    if step < SUBSTEPS - 1:
        g_ref, vw_ref, adv_ref, send_ref, rhs, packed, sems = refs
    else:
        g_ref, vw_ref, send_ref, rhs = refs
        adv_ref = None
    own = lax.axis_index("gy")
    odd = lax.rem(lax.axis_index("gx"), 2) > 0
    stiff = stiff_ref[0]

    for r in range(0, CY, CHUNK):
        rows = slice(r, r + CHUNK)
        plus = [2.0 * courant[0] * jnp.maximum(u_ref[0, x, rows, :], 0.0) for x in range(2)]
        minus = [2.0 * courant[0] * jnp.minimum(u_ref[0, x, rows, :], 0.0) for x in range(2)]
        if step > 0:
            v, w = old_vw[0, rows, :], old_vw[1, rows, :]
        for c in range(3):
            away = [far[c, x, rows, :] for x in range(2)]
            if step > 0:
                for x in range(2):
                    line = 2 * c + x
                    away[x] = away[x] - v * far_lf[0, line : line + 1, :] - w * far_lf[1, line : line + 1, :]
            close = [near[c, x, rows, :] for x in range(2)]
            low = [jnp.where(odd, close[x], away[x]) for x in range(2)]
            high = [jnp.where(odd, away[x], close[x]) for x in range(2)]
            along = low + [u_ref[c, 0, rows, :], u_ref[c, 1, rows, :]] + high
            for x in range(2):
                b2, b1, a1, a2 = along[x], along[x + 1], along[x + 3], along[x + 4]
                adv = plus[x] * (0.25 * b2 - b1) + minus[x] * (a1 - 0.25 * a2)
                column = (2 * c + x) * LANES
                rhs[rows, column : column + LANES] = part_ref[c, x, rows, :] - new_weight[step] * adv
                if adv_ref is not None:
                    adv_ref[c, x, rows, :] = adv

    if step == 0:
        for c, x in lines():
            low, high = before[c, x], behind[c, x]
            y2, y1, w1, w2 = low[6:7], low[7:8], high[0:1], high[1:2]
            for row, viscous, up, down in (
                (0, y1, 0.25 * y2 - y1, None),
                (1, None, 0.25 * y1, None),
                (CY - 2, None, None, -0.25 * w1),
                (CY - 1, w1, None, w1 - 0.25 * w2),
            ):
                speed = u_ref[1, x, row : row + 1, :]
                if up is not None:
                    adv = 2.0 * courant[1] * jnp.maximum(speed, 0.0) * up
                else:
                    adv = 2.0 * courant[1] * jnp.minimum(speed, 0.0) * down
                adv_ref[c, x, row : row + 1, :] = adv_ref[c, x, row : row + 1, :] + adv
                change = -new_weight[step] * adv
                if viscous is not None:
                    change = change + (implicit_share[step] * stiff) * viscous
                column = slice((2 * c + x) * LANES, (2 * c + x + 1) * LANES)
                rhs[row : row + 1, column] = rhs[row : row + 1, column] + change

    inverse = inv_ref[...]
    first_flag = jnp.where(own > 0, 1.0, 0.0)
    last_flag = jnp.where(own < 7, 1.0, 0.0)
    coupling = -implicit_share[step] * stiff
    vw_ref[0] = jnp.broadcast_to(inverse[:, 0:1] * (coupling * first_flag), (CY, LANES))
    vw_ref[1] = jnp.broadcast_to(inverse[:, CY - 1 : CY] * (coupling * last_flag), (CY, LANES))

    def product(some, pair):
        return jnp.dot(
            some,
            rhs[:, pair * 256 : pair * 256 + 256],
            precision=lax.Precision.HIGHEST,
            preferred_element_type=jnp.float32,
        )

    def tile(row, pick):
        picked = [pick(c, x, row) for c, x in lines()]
        return jnp.concatenate(picked + [vw_ref[0, row : row + 1, :], vw_ref[1, row : row + 1, :]], axis=0)

    if adv_ref is not None:
        outer = jnp.concatenate([inverse[0:8], inverse[CY - 8 : CY]], axis=0)
        found = [product(outer, pair) for pair in range(3)]

        def outermost(c, x, row):
            at = row if row < 8 else row - CY + 16
            return found[c][at : at + 1, x * LANES : (x + 1) * LANES]

        for way, beside in enumerate((1, CY - 2)):
            for t, row in enumerate((0, CY - 1, beside)):
                packed[way, t] = tile(row, outermost)
        copies = [
            pltpu.make_async_copy(packed.at[jnp.where(own < dest, 1, 0)], send_ref.at[dest], sems.at[dest])
            for dest in range(8)
        ]
        for copy in copies:
            copy.start()

        @pl.when(own >= 0)
        def _():
            for pair in range(3):
                solved = product(inv_ref[...], pair)
                g_ref[pair, 0] = solved[:, :LANES]
                g_ref[pair, 1] = solved[:, LANES:]

        for copy in copies:
            copy.wait()
    else:
        for pair in range(3):
            solved = product(inverse, pair)
            g_ref[pair, 0] = solved[:, :LANES]
            g_ref[pair, 1] = solved[:, LANES:]
        for t, row in enumerate((0, CY - 1)):
            ends = tile(row, lambda c, x, row: g_ref[c, x, row : row + 1, :])
            for dest in range(8):
                send_ref[dest, t] = ends


def correct_kernel(step, got, g_ref, vw_ref, *refs):
    if step < SUBSTEPS - 1:
        u_ref, ends_ref, lf_ref, heads, tails = refs
    else:
        out_ref, heads, tails, u_ref, sems = refs
        ends_ref = None
    own = lax.axis_index("gy")
    shape = (8, LANES)
    zero = jnp.zeros(shape, jnp.float32)

    def tip(block, t, which):
        return jnp.broadcast_to(got[block, t, 6 + which : 7 + which, :], shape)

    for edge in (0, 1, 10, 11):
        heads[edge] = zero
        tails[edge] = zero
    prev_q, prev_last = zero, zero
    fronts, backs, front_qs, back_qs = [], [], [], []
    for block in range(8):
        head_v, tail_v, head_w, tail_w = tip(block, 0, 0), tip(block, 1, 0), tip(block, 0, 1), tip(block, 1, 1)
        pivot = 1.0 / (1.0 - head_v * prev_q)
        front = (got[block, 0] - head_v * prev_last) * pivot
        back = got[block, 1] - tail_v * prev_last + tail_v * prev_q * front
        front_q = head_w * pivot
        back_q = tail_w + tail_v * prev_q * front_q
        fronts.append(front)
        backs.append(back)
        front_qs.append(front_q)
        back_qs.append(back_q)
        prev_q, prev_last = back_q, back
    after = zero
    for block in range(7, -1, -1):
        head = fronts[block] - front_qs[block] * after
        heads[block + 2] = head
        tails[block + 2] = backs[block] - back_qs[block] * after
        after = head

    lower = tails[own + 1]
    upper = heads[own + 3]
    for c in range(3):
        for x in range(2):
            line = 2 * c + x
            low = lower[line : line + 1, :]
            high = upper[line : line + 1, :]
            u_ref[c, x] = g_ref[c, x] - vw_ref[0] * low - vw_ref[1] * high
        if ends_ref is None:
            pltpu.make_async_copy(u_ref.at[c], out_ref.at[c], sems.at[c]).start()
    if ends_ref is None:
        for c in range(3):
            pltpu.make_async_copy(u_ref.at[c], out_ref.at[c], sems.at[c]).wait()
    if ends_ref is not None:
        lf_ref[0] = lower
        lf_ref[1] = upper
        before = jnp.maximum(own - 1, 0)
        behind = jnp.minimum(own + 1, 7)
        row = got[before, 2]
        row = row - jnp.broadcast_to(got[before, 2, 6:7, :], shape) * tails[own]
        row = row - jnp.broadcast_to(got[before, 2, 7:8, :], shape) * heads[own + 2]
        ends_ref[0] = jnp.where(own > 0, row, zero)
        ends_ref[1] = lower
        ends_ref[2] = upper
        row = got[behind, 2]
        row = row - jnp.broadcast_to(got[behind, 2, 6:7, :], shape) * tails[own + 2]
        row = row - jnp.broadcast_to(got[behind, 2, 7:8, :], shape) * heads[own + 4]
        ends_ref[3] = jnp.where(own < 7, row, zero)


def f32(*shape):
    return pltpu.VMEM(shape, jnp.float32)


def call(kernel, arrays, outs, scratch, flops, scalars=(), large=(), hbm_outs=0):
    return pl.pallas_call(
        kernel,
        out_shape=outs,
        in_specs=[SMEM] * len(scalars) + [HBM] * len(large) + [VMEM] * len(arrays),
        out_specs=[VMEM] * (len(outs) - hbm_outs) + [HBM] * hbm_outs,
        scratch_shapes=scratch,
        cost_estimate=pl.CostEstimate(flops=flops, bytes_accessed=4 << 20, transcendentals=0),
        compiler_params=pltpu.CompilerParams(vmem_limit_bytes=16 << 20),
    )(
        *scalars,
        *[pltpu.with_memory_space_constraint(a, pltpu.HBM) for a in large],
        *[pltpu.with_memory_space_constraint(a, pltpu.VMEM) for a in arrays],
    )


def exchange(send):
    flat = send.reshape(8, send.shape[1] * 8, LANES)
    return lax.all_to_all(flat, "gy", split_axis=0, concat_axis=0).reshape(send.shape)


def scratch(*shape):
    return pltpu.VMEM(shape, jnp.float32)


def body(velocity, stiffness, block_inverse):
    gx = lax.axis_size("gx")
    gy = lax.axis_size("gy")
    field = f32(3, 2, CY, LANES)
    across = swaps(gx, 1, True)
    inside = swaps(gx, 0, True)
    for step in range(SUBSTEPS):
        last = step == SUBSTEPS - 1
        if step == 0:
            far = lax.ppermute(velocity, "gx", across)
            outs = [field] + [f32(3, 2, 8, LANES)] * 2
            current, top, bottom = call(pack_kernel, [], outs, [pltpu.SemaphoreType.DMA((3,))], 10**6, large=[velocity])
            before = lax.ppermute(bottom, "gy", [(k, k + 1) for k in range(gy - 1)])
            behind = lax.ppermute(top, "gy", [(k + 1, k) for k in range(gy - 1)])
            own_args = [current]
            more_args = [before, behind]
        else:
            far_lf = lax.ppermute(lf, "gx", across)
            own_args = [current, ends, share, adv]
            more_args = [far_lf, vw]
        near = lax.ppermute(current, "gx", inside)
        pad = [scratch(3, 2, CY + 16, LANES), pltpu.SemaphoreType.DMA]
        own = functools.partial(own_kernel, step)
        outs = [field, f32(CY, CY)] + [field] * (0 if last else 1)
        part, inverse, *shares = call(own, own_args, outs, pad, 10**8, [stiffness], [block_inverse])
        arrays = [current, far, near, part, inverse] + more_args
        planes = functools.partial(planes_kernel, step)
        edge = [scratch(CY, 6 * LANES)]
        if last:
            outs = [field, f32(2, CY, LANES), f32(8, 2, 8, LANES)]
        else:
            outs = [field, f32(2, CY, LANES), field, jax.ShapeDtypeStruct((8, 3, 8, LANES), jnp.float32)]
            edge += [scratch(2, 3, 8, LANES), pltpu.SemaphoreType.DMA((8,))]
        results = call(planes, arrays, outs, edge, 10**9, [stiffness], hbm_outs=0 if last else 1)
        g, vw, *advs, send = results
        got = exchange(send)
        if not last:
            share, adv = shares[0], advs[0]
            far = lax.ppermute(g, "gx", across)
        correct = functools.partial(correct_kernel, step)
        edge = [scratch(12, 8, LANES)] * 2
        if last:
            outs = [jax.ShapeDtypeStruct((3, 2, CY, LANES), jnp.float32)]
            edge = edge + [scratch(3, 2, CY, LANES), pltpu.SemaphoreType.DMA((3,))]
            return call(correct, [got, g, vw], outs, edge, 10**8, hbm_outs=1)[0]
        outs = [field, f32(4, 8, LANES), f32(2, 8, LANES)]
        current, ends, lf = call(correct, [got, g, vw], outs, edge, 10**8)


def solution(mesh):
    return jax.shard_map(
        body,
        mesh=mesh,
        in_specs=(P(None, "gx", "gy", None), P("gy"), P(None, "gy", None)),
        out_specs=P(None, "gx", "gy", None),
        check_vma=False,
    )
```

```python
import functools

import jax
import jax.numpy as jnp
from jax import lax
from jax.experimental import pallas as pl
from jax.experimental.pallas import tpu as pltpu
from jax.sharding import PartitionSpec as P


SUBSTEPS = 3
implicit_share = (8.0 / 15.0, 2.0 / 15.0, 1.0 / 3.0)
new_weight = (8.0 / 15.0, 5.0 / 12.0, 3.0 / 4.0)
old_weight = (0.0, -17.0 / 60.0, -5.0 / 12.0)
courant = (0.3, 0.2, 0.3)

CY = 192
LANES = 128
CHUNK = 32

VMEM = pl.BlockSpec(memory_space=pltpu.VMEM)
HBM = pl.BlockSpec(memory_space=pltpu.HBM)
SMEM = pl.BlockSpec(memory_space=pltpu.SMEM)


def swaps(count, offset, closed):
    pairs = []
    for a in range(offset, count + offset - 1, 2):
        b = a + 1
        if b < count:
            pairs += [(a, b), (b, a)]
        elif closed:
            pairs += [(a, 0), (0, a)]
    return pairs


def lines():
    return [(c, x) for c in range(3) for x in range(2)]


def pack_kernel(velocity, u_ref, rows_ref, sems):
    copies = [
        pltpu.make_async_copy(velocity.at[:, :, pl.ds(0, 8), :], rows_ref.at[:, :, pl.ds(0, 8), :], sems.at[0]),
        pltpu.make_async_copy(velocity.at[:, :, pl.ds(CY - 8, 8), :], rows_ref.at[:, :, pl.ds(8, 8), :], sems.at[1]),
        pltpu.make_async_copy(velocity, u_ref, sems.at[2]),
    ]
    for copy in copies:
        copy.start()
    for copy in copies:
        copy.wait()


def own_kernel(step, *refs):
    if step == 0:
        stiff_ref, inverses, u_ref, *refs = refs
        ends_ref = old_ref = None
    else:
        stiff_ref, inverses, u_ref, ends_ref, old_share, old_ref, *refs = refs
    if step < SUBSTEPS - 1:
        part_ref, inv_ref, share_ref, pad, sem = refs
    else:
        part_ref, inv_ref, pad, sem = refs
        share_ref = None
    fetch = pltpu.make_async_copy(inverses.at[step], inv_ref, sem)
    fetch.start()
    stiff = stiff_ref[0]

    for c in range(3):
        for x in range(2):
            pad[c, x, 8 : 8 + CY, :] = u_ref[c, x]
            if step == 0:
                pad[c, x, 0:8, :] = jnp.zeros((8, LANES), jnp.float32)
                pad[c, x, 8 + CY : 16 + CY, :] = jnp.zeros((8, LANES), jnp.float32)
            else:
                line = 2 * c + x
                pad[c, x, 6:7, :] = ends_ref[0, line : line + 1, :]
                pad[c, x, 7:8, :] = ends_ref[1, line : line + 1, :]
                pad[c, x, 8 + CY : 9 + CY, :] = ends_ref[2, line : line + 1, :]
                pad[c, x, 9 + CY : 10 + CY, :] = ends_ref[3, line : line + 1, :]

    for r in range(0, CY, CHUNK):
        rows = slice(r, r + CHUNK)
        for x in range(2):
            speed = [u_ref[d, x, rows, :] for d in range(3)]
            plus = [2.0 * courant[d] * jnp.maximum(speed[d], 0.0) for d in range(3)]
            minus = [2.0 * courant[d] * jnp.minimum(speed[d], 0.0) for d in range(3)]
            total = plus[0] - minus[0]
            for d in (1, 2):
                total = total + (plus[d] - minus[d])
            total = 0.75 * total
            for c in range(3):
                f = speed[c]
                adv = total * f
                y2, y1 = pad[c, x, 6 + r : 6 + r + CHUNK, :], pad[c, x, 7 + r : 7 + r + CHUNK, :]
                w1, w2 = pad[c, x, 9 + r : 9 + r + CHUNK, :], pad[c, x, 10 + r : 10 + r + CHUNK, :]
                adv = adv + plus[1] * (0.25 * y2 - y1) + minus[1] * (w1 - 0.25 * w2)
                z1, z2 = pltpu.roll(f, 1, 1), pltpu.roll(f, 2, 1)
                t1, t2 = pltpu.roll(f, LANES - 1, 1), pltpu.roll(f, LANES - 2, 1)
                adv = adv + plus[2] * (0.25 * z2 - z1) + minus[2] * (t1 - 0.25 * t2)
                forcing = f + (implicit_share[step] * stiff) * (w1 - 2.0 * f + y1) - new_weight[step] * adv
                if old_ref is not None:
                    old = old_share[c, x, rows, :] + old_ref[c, x, rows, :]
                    forcing = forcing - old_weight[step] * old
                part_ref[c, x, rows, :] = forcing
                if share_ref is not None:
                    share_ref[c, x, rows, :] = adv
    fetch.wait()


def planes_kernel(step, *refs):
    stiff_ref, u_ref, far, near, part_ref, inv_ref, *refs = refs
    if step > 0:
        far_lf, old_vw, *refs = refs
    else:
        pair_y, other_y, *refs = refs
    if step < SUBSTEPS - 1:
        g_ref, vw_ref, adv_ref, send_ref, rhs, packed, sems = refs
    else:
        g_ref, vw_ref, send_ref, rhs = refs
        adv_ref = None
    own = lax.axis_index("gy")
    odd = lax.rem(lax.axis_index("gx"), 2) > 0
    stiff = stiff_ref[0]

    for r in range(0, CY, CHUNK):
        rows = slice(r, r + CHUNK)
        plus = [2.0 * courant[0] * jnp.maximum(u_ref[0, x, rows, :], 0.0) for x in range(2)]
        minus = [2.0 * courant[0] * jnp.minimum(u_ref[0, x, rows, :], 0.0) for x in range(2)]
        if step > 0:
            v, w = old_vw[0, rows, :], old_vw[1, rows, :]
        for c in range(3):
            away = [far[c, x, rows, :] for x in range(2)]
            if step > 0:
                for x in range(2):
                    line = 2 * c + x
                    away[x] = away[x] - v * far_lf[0, line : line + 1, :] - w * far_lf[1, line : line + 1, :]
            close = [near[c, x, rows, :] for x in range(2)]
            low = [jnp.where(odd, close[x], away[x]) for x in range(2)]
            high = [jnp.where(odd, away[x], close[x]) for x in range(2)]
            along = low + [u_ref[c, 0, rows, :], u_ref[c, 1, rows, :]] + high
            for x in range(2):
                b2, b1, a1, a2 = along[x], along[x + 1], along[x + 3], along[x + 4]
                adv = plus[x] * (0.25 * b2 - b1) + minus[x] * (a1 - 0.25 * a2)
                column = (2 * c + x) * LANES
                rhs[rows, column : column + LANES] = part_ref[c, x, rows, :] - new_weight[step] * adv
                if adv_ref is not None:
                    adv_ref[c, x, rows, :] = adv

    if step == 0:
        odd_y = lax.rem(own, 2) > 0
        for c, x in lines():
            low = jnp.where(odd_y, pair_y[c, x, 8:16, :], other_y[c, x, 8:16, :])
            high = jnp.where(odd_y, other_y[c, x, 0:8, :], pair_y[c, x, 0:8, :])
            y2, y1, w1, w2 = low[6:7], low[7:8], high[0:1], high[1:2]
            for row, viscous, up, down in (
                (0, y1, 0.25 * y2 - y1, None),
                (1, None, 0.25 * y1, None),
                (CY - 2, None, None, -0.25 * w1),
                (CY - 1, w1, None, w1 - 0.25 * w2),
            ):
                speed = u_ref[1, x, row : row + 1, :]
                if up is not None:
                    adv = 2.0 * courant[1] * jnp.maximum(speed, 0.0) * up
                else:
                    adv = 2.0 * courant[1] * jnp.minimum(speed, 0.0) * down
                adv_ref[c, x, row : row + 1, :] = adv_ref[c, x, row : row + 1, :] + adv
                change = -new_weight[step] * adv
                if viscous is not None:
                    change = change + (implicit_share[step] * stiff) * viscous
                column = slice((2 * c + x) * LANES, (2 * c + x + 1) * LANES)
                rhs[row : row + 1, column] = rhs[row : row + 1, column] + change

    inverse = inv_ref[...]
    first_flag = jnp.where(own > 0, 1.0, 0.0)
    last_flag = jnp.where(own < 7, 1.0, 0.0)
    coupling = -implicit_share[step] * stiff
    vw_ref[0] = jnp.broadcast_to(inverse[:, 0:1] * (coupling * first_flag), (CY, LANES))
    vw_ref[1] = jnp.broadcast_to(inverse[:, CY - 1 : CY] * (coupling * last_flag), (CY, LANES))

    def product(some, pair):
        return jnp.dot(
            some,
            rhs[:, pair * 256 : pair * 256 + 256],
            precision=lax.Precision.HIGHEST,
            preferred_element_type=jnp.float32,
        )

    def tile(row, pick):
        picked = [pick(c, x, row) for c, x in lines()]
        return jnp.concatenate(picked + [vw_ref[0, row : row + 1, :], vw_ref[1, row : row + 1, :]], axis=0)

    if adv_ref is not None:
        outer = jnp.concatenate([inverse[0:8], inverse[CY - 8 : CY]], axis=0)
        found = [product(outer, pair) for pair in range(3)]

        def outermost(c, x, row):
            at = row if row < 8 else row - CY + 16
            return found[c][at : at + 1, x * LANES : (x + 1) * LANES]

        for way, beside in enumerate((1, CY - 2)):
            for t, row in enumerate((0, CY - 1, beside)):
                packed[way, t] = tile(row, outermost)
        copies = [
            pltpu.make_async_copy(packed.at[jnp.where(own < dest, 1, 0)], send_ref.at[dest], sems.at[dest])
            for dest in range(8)
        ]
        for copy in copies:
            copy.start()

        @pl.when(own >= 0)
        def _():
            for pair in range(3):
                solved = product(inv_ref[...], pair)
                g_ref[pair, 0] = solved[:, :LANES]
                g_ref[pair, 1] = solved[:, LANES:]

        for copy in copies:
            copy.wait()
    else:
        for pair in range(3):
            solved = product(inverse, pair)
            g_ref[pair, 0] = solved[:, :LANES]
            g_ref[pair, 1] = solved[:, LANES:]
        for t, row in enumerate((0, CY - 1)):
            ends = tile(row, lambda c, x, row: g_ref[c, x, row : row + 1, :])
            for dest in range(8):
                send_ref[dest, t] = ends


def correct_kernel(step, got, g_ref, vw_ref, *refs):
    if step < SUBSTEPS - 1:
        u_ref, ends_ref, lf_ref, heads, tails = refs
    else:
        out_ref, heads, tails, u_ref, sems = refs
        ends_ref = None
    own = lax.axis_index("gy")
    shape = (8, LANES)
    zero = jnp.zeros(shape, jnp.float32)

    def tip(block, t, which):
        return jnp.broadcast_to(got[block, t, 6 + which : 7 + which, :], shape)

    for edge in (0, 1, 10, 11):
        heads[edge] = zero
        tails[edge] = zero
    prev_q, prev_last = zero, zero
    fronts, backs, front_qs, back_qs = [], [], [], []
    for block in range(8):
        head_v, tail_v, head_w, tail_w = tip(block, 0, 0), tip(block, 1, 0), tip(block, 0, 1), tip(block, 1, 1)
        pivot = 1.0 / (1.0 - head_v * prev_q)
        front = (got[block, 0] - head_v * prev_last) * pivot
        back = got[block, 1] - tail_v * prev_last + tail_v * prev_q * front
        front_q = head_w * pivot
        back_q = tail_w + tail_v * prev_q * front_q
        fronts.append(front)
        backs.append(back)
        front_qs.append(front_q)
        back_qs.append(back_q)
        prev_q, prev_last = back_q, back
    after = zero
    for block in range(7, -1, -1):
        head = fronts[block] - front_qs[block] * after
        heads[block + 2] = head
        tails[block + 2] = backs[block] - back_qs[block] * after
        after = head

    lower = tails[own + 1]
    upper = heads[own + 3]
    for c in range(3):
        for x in range(2):
            line = 2 * c + x
            low = lower[line : line + 1, :]
            high = upper[line : line + 1, :]
            u_ref[c, x] = g_ref[c, x] - vw_ref[0] * low - vw_ref[1] * high
            if ends_ref is None:
                pltpu.make_async_copy(u_ref.at[c, x], out_ref.at[c, x], sems.at[line]).start()
    if ends_ref is None:
        for c, x in lines():
            pltpu.make_async_copy(u_ref.at[c, x], out_ref.at[c, x], sems.at[2 * c + x]).wait()
    if ends_ref is not None:
        lf_ref[0] = lower
        lf_ref[1] = upper
        before = jnp.maximum(own - 1, 0)
        behind = jnp.minimum(own + 1, 7)
        row = got[before, 2]
        row = row - jnp.broadcast_to(got[before, 2, 6:7, :], shape) * tails[own]
        row = row - jnp.broadcast_to(got[before, 2, 7:8, :], shape) * heads[own + 2]
        ends_ref[0] = jnp.where(own > 0, row, zero)
        ends_ref[1] = lower
        ends_ref[2] = upper
        row = got[behind, 2]
        row = row - jnp.broadcast_to(got[behind, 2, 6:7, :], shape) * tails[own + 2]
        row = row - jnp.broadcast_to(got[behind, 2, 7:8, :], shape) * heads[own + 4]
        ends_ref[3] = jnp.where(own < 7, row, zero)


def f32(*shape):
    return pltpu.VMEM(shape, jnp.float32)


def call(kernel, arrays, outs, scratch, flops, scalars=(), large=(), hbm_outs=0):
    return pl.pallas_call(
        kernel,
        out_shape=outs,
        in_specs=[SMEM] * len(scalars) + [HBM] * len(large) + [VMEM] * len(arrays),
        out_specs=[VMEM] * (len(outs) - hbm_outs) + [HBM] * hbm_outs,
        scratch_shapes=scratch,
        cost_estimate=pl.CostEstimate(flops=flops, bytes_accessed=4 << 20, transcendentals=0),
        compiler_params=pltpu.CompilerParams(vmem_limit_bytes=16 << 20),
    )(
        *scalars,
        *[pltpu.with_memory_space_constraint(a, pltpu.HBM) for a in large],
        *[pltpu.with_memory_space_constraint(a, pltpu.VMEM) for a in arrays],
    )


def exchange(send):
    flat = send.reshape(8, send.shape[1] * 8, LANES)
    return lax.all_to_all(flat, "gy", split_axis=0, concat_axis=0).reshape(send.shape)


def scratch(*shape):
    return pltpu.VMEM(shape, jnp.float32)


def body(velocity, stiffness, block_inverse):
    gx = lax.axis_size("gx")
    gy = lax.axis_size("gy")
    field = f32(3, 2, CY, LANES)
    across = swaps(gx, 1, True)
    inside = swaps(gx, 0, True)
    for step in range(SUBSTEPS):
        last = step == SUBSTEPS - 1
        if step == 0:
            far = lax.ppermute(velocity, "gx", across)
            outs = [field, f32(3, 2, 16, LANES)]
            current, rows = call(pack_kernel, [], outs, [pltpu.SemaphoreType.DMA((3,))], 10**6, large=[velocity])
            pair_y = lax.ppermute(rows, "gy", swaps(gy, 0, False))
            other_y = lax.ppermute(rows, "gy", swaps(gy, 1, False))
            own_args = [current]
            more_args = [pair_y, other_y]
        else:
            far_lf = lax.ppermute(lf, "gx", across)
            own_args = [current, ends, share, adv]
            more_args = [far_lf, vw]
        near = lax.ppermute(current, "gx", inside)
        pad = [scratch(3, 2, CY + 16, LANES), pltpu.SemaphoreType.DMA]
        own = functools.partial(own_kernel, step)
        outs = [field, f32(CY, CY)] + [field] * (0 if last else 1)
        part, inverse, *shares = call(own, own_args, outs, pad, 10**8, [stiffness], [block_inverse])
        arrays = [current, far, near, part, inverse] + more_args
        planes = functools.partial(planes_kernel, step)
        edge = [scratch(CY, 6 * LANES)]
        if last:
            outs = [field, f32(2, CY, LANES), f32(8, 2, 8, LANES)]
        else:
            outs = [field, f32(2, CY, LANES), field, jax.ShapeDtypeStruct((8, 3, 8, LANES), jnp.float32)]
            edge += [scratch(2, 3, 8, LANES), pltpu.SemaphoreType.DMA((8,))]
        results = call(planes, arrays, outs, edge, 10**9, [stiffness], hbm_outs=0 if last else 1)
        g, vw, *advs, send = results
        got = exchange(send)
        if not last:
            share, adv = shares[0], advs[0]
            far = lax.ppermute(g, "gx", across)
        correct = functools.partial(correct_kernel, step)
        edge = [scratch(12, 8, LANES)] * 2
        if last:
            outs = [jax.ShapeDtypeStruct((3, 2, CY, LANES), jnp.float32)]
            edge = edge + [scratch(3, 2, CY, LANES), pltpu.SemaphoreType.DMA((6,))]
            return call(correct, [got, g, vw], outs, edge, 10**8, hbm_outs=1)[0]
        outs = [field, f32(4, 8, LANES), f32(2, 8, LANES)]
        current, ends, lf = call(correct, [got, g, vw], outs, edge, 10**8)


def solution(mesh):
    return jax.shard_map(
        body,
        mesh=mesh,
        in_specs=(P(None, "gx", "gy", None), P("gy"), P(None, "gy", None)),
        out_specs=P(None, "gx", "gy", None),
        check_vma=False,
    )
```
